256 devices in a mesh: filt: 32 (over y, z_hi, core), space: 8 (over z_lo, x).
Axes of the slice: x: 4, y: 4, z: 8 (z_hi: 4, z_lo: 2; z = z_hi * 2 + z_lo), core: 2. Of those that a mesh axis runs over, the one named last changes fastest.
Arguments:
- volume: bfloat16 [256, 32, 4, 128], P('filt', 'space'), may hold values from -6 to 6
- kernel: bfloat16 [512, 3, 3, 3, 256], P('filt'), may hold values from -0.078125 to 0.078125
- filter_bias: bfloat16 [512], P('filt'), may hold values from -3 to 3
Outputs:
- pooled: bfloat16 [512, 16, 2, 64], P('filt', 'space')
The draws below stay inside these ranges and needn't reach their ends.
All inputs are finite; a program needn't handle non-finite values.
Results may differ from the reference program's by a relative error of at most 0.001.
Values may be sent and summed in bfloat16 or wider, within the bound.
A program may use at most 64 MiB of HBM per device.

```python
import jax
import jax.numpy as jnp
from jax import lax

CIN = 256
COUT = 512
NY = 4
NX = 128
NZ = 32


def block_scale(rng, extent, pieces, least, largest):
    gain = 1.0
    for dim, blocks in pieces:
        draws = jax.random.uniform(jax.random.fold_in(jax.random.fold_in(rng, 6), dim), (blocks,), jnp.float32, least / len(pieces), largest / len(pieces))
        gain = gain * jnp.repeat(jnp.exp(draws), extent[dim] // blocks).reshape((-1,) + (1,) * (len(extent) - 1 - dim))
    return gain


def bell_draw(own_key, dims, deviation, reach, split=(), held_as=jnp.bfloat16):
    level = block_scale(own_key, dims, split, -0.22, 0.18) if split else 1.0
    result = jax.random.normal(own_key, dims, jnp.float32) * deviation * level
    return jnp.minimum(jnp.maximum(result, -reach), reach).astype(held_as)


def setup_inputs(seed: int = 0) -> dict:
    splits = jax.random.split(jax.random.key(seed), 4)
    return {
        "volume": bell_draw(splits[0], (CIN, NZ, NY, NX), 1.0, 6.0, ((0, 32), (1, 8))),
        "kernel": bell_draw(splits[1], (COUT, 3, 3, 3, CIN), (27 * CIN) ** -0.5, 0.078125, ((0, 32),)),
        "filter_bias": bell_draw(splits[2], (COUT,), 0.5, 3.0, ((0, 32),)),
    }


slope = 0.3


def reference(volume, kernel, filter_bias):
    inputs = volume.astype(jnp.float32)[None]
    weights = kernel.astype(jnp.float32)
    summed = lax.conv_general_dilated(inputs, weights, (1, 1, 1), ((1, 1), (1, 1), (1, 1)), dimension_numbers=("NCDHW", "ODHWI", "NCDHW"), precision=lax.Precision.HIGHEST)[0]
    activated = summed + filter_bias.astype(jnp.float32)[:, None, None, None]
    activated = jnp.where(activated > 0, activated, slope * activated)
    filters, depth, height, across = activated.shape
    blocked = activated.reshape(filters, depth // 2, 2, height // 2, 2, across // 2, 2)
    return jnp.max(blocked, axis=(2, 4, 6)).astype(jnp.bfloat16)
```

```python
import functools

import jax
import jax.numpy as jnp
from jax import lax
from jax.experimental import pallas as pl
from jax.experimental.pallas import tpu as pltpu
from jax.sharding import PartitionSpec as P

slope = 0.3
MESH = pl.DeviceIdType.MESH


def with_halo(block, sides, width):
    for axis, dim in sides:
        count = lax.axis_size(axis)
        forward = [(i, i + 1) for i in range(count - 1)]
        backward = [(target, source) for source, target in forward]
        low = lax.ppermute(
            lax.slice_in_dim(block, block.shape[dim] - width, None, axis=dim), axis, forward
        )
        high = lax.ppermute(lax.slice_in_dim(block, 0, width, axis=dim), axis, backward)
        block = jnp.concatenate([low, block, high], axis=dim)
    return block


def gather_kernel(n, x_ref, out_ref, local_sem, send_sem, recv_sem):
    me = lax.axis_index("filt")
    sp = lax.axis_index("space")
    barrier = pltpu.get_barrier_semaphore()
    for k in range(1, n):
        peer = lax.rem(me + k, n)
        pl.semaphore_signal(barrier, inc=1, device_id=(peer, sp), device_id_type=MESH)
    pl.semaphore_wait(barrier, n - 1)

    local = pltpu.make_async_copy(x_ref, out_ref.at[me], local_sem.at[0])
    local.start()
    copies = []
    for k in range(1, n):
        peer = lax.rem(me + k, n)
        copy = pltpu.make_async_remote_copy(
            src_ref=x_ref,
            dst_ref=out_ref.at[me],
            send_sem=send_sem.at[k],
            recv_sem=recv_sem.at[me],
            device_id=(peer, sp),
            device_id_type=MESH,
        )
        copy.start()
        copies.append(copy)
    for k in range(1, n):
        copies[k - 1].wait_send()
    for k in range(1, n):
        src = lax.rem(me + n - k, n)
        pltpu.make_async_remote_copy(
            src_ref=x_ref,
            dst_ref=out_ref.at[src],
            send_sem=send_sem.at[k],
            recv_sem=recv_sem.at[src],
            device_id=(src, sp),
            device_id_type=MESH,
        ).wait_recv()
    local.wait()


def gather_filt(block):
    n = lax.axis_size("filt")
    return pl.pallas_call(
        functools.partial(gather_kernel, n),
        out_shape=jax.ShapeDtypeStruct((n,) + block.shape, block.dtype),
        in_specs=[pl.BlockSpec(memory_space=pl.ANY)],
        out_specs=pl.BlockSpec(memory_space=pl.ANY),
        scratch_shapes=[
            pltpu.SemaphoreType.DMA((1,)),
            pltpu.SemaphoreType.DMA((n,)),
            pltpu.SemaphoreType.DMA((n,)),
        ],
        compiler_params=pltpu.CompilerParams(collective_id=0, has_side_effects=True),
    )(block)


def convolve(inputs, weights, padding):
    return lax.conv_general_dilated(
        inputs[None],
        weights,
        (1, 1, 1),
        padding,
        dimension_numbers=("NCDHW", "ODHWI", "NCDHW"),
        preferred_element_type=jnp.float32,
    )[0]


def finish(summed, filter_bias):
    activated = summed + filter_bias.astype(jnp.float32)[:, None, None, None]
    activated = jnp.where(activated > 0, activated, slope * activated)
    filters, depth, height, across = activated.shape
    blocked = activated.reshape(filters, depth // 2, 2, height // 2, 2, across // 2, 2)
    return jnp.max(blocked, axis=(2, 4, 6)).astype(jnp.bfloat16)


def on_device(volume, kernel, filter_bias):
    padded = with_halo(volume, (("space", 1),), 1)
    gathered = gather_filt(padded)
    gathered = gathered.reshape((-1,) + gathered.shape[2:])
    summed = convolve(gathered, kernel, ((0, 0), (1, 1), (1, 1)))
    return finish(summed, filter_bias)


def solution(mesh):
    in_specs = (P("filt", "space", None, None), P("filt", None, None, None, None), P("filt"))
    out_specs = P("filt", "space", None, None)
    return jax.shard_map(
        on_device, mesh=mesh, in_specs=in_specs, out_specs=out_specs, check_vma=False
    )
```

```python
import functools

import jax
import jax.numpy as jnp
from jax import lax
from jax.experimental import pallas as pl
from jax.experimental.pallas import tpu as pltpu
from jax.sharding import PartitionSpec as P

slope = 0.3
MESH = pl.DeviceIdType.MESH


def with_halo(block, sides, width):
    for axis, dim in sides:
        count = lax.axis_size(axis)
        forward = [(i, i + 1) for i in range(count - 1)]
        backward = [(target, source) for source, target in forward]
        low = lax.ppermute(
            lax.slice_in_dim(block, block.shape[dim] - width, None, axis=dim), axis, forward
        )
        high = lax.ppermute(lax.slice_in_dim(block, 0, width, axis=dim), axis, backward)
        block = jnp.concatenate([low, block, high], axis=dim)
    return block


def gather_kernel(n, x_ref, out_ref, local_sem, send_sem, fwd_sem, recv_sem):
    me = lax.axis_index("filt")
    sp = lax.axis_index("space")
    chips = n // 2
    core = lax.rem(me, 2)
    chip = me // 2
    sib = me + 1 - 2 * core
    peers = [lax.rem(chip + k, chips) * 2 + core for k in range(1, chips)]
    sources = [lax.rem(chip + chips - k, chips) * 2 + core for k in range(1, chips)]

    barrier = pltpu.get_barrier_semaphore()
    for peer in [sib] + peers:
        pl.semaphore_signal(barrier, inc=1, device_id=(peer, sp), device_id_type=MESH)
    pl.semaphore_wait(barrier, chips)

    def remote(src, dst_slot, sem, dev):
        return pltpu.make_async_remote_copy(
            src_ref=src,
            dst_ref=out_ref.at[dst_slot],
            send_sem=sem,
            recv_sem=recv_sem.at[dst_slot],
            device_id=(dev, sp),
            device_id_type=MESH,
        )

    local = pltpu.make_async_copy(x_ref, out_ref.at[me], local_sem.at[0])
    local.start()
    sends = [remote(x_ref, me, send_sem.at[0], sib)]
    for k, peer in enumerate(peers):
        sends.append(remote(x_ref, me, send_sem.at[k + 1], peer))
    for copy in sends:
        copy.start()
    forwards = []
    for k, src in enumerate(sources):
        remote(out_ref.at[src], src, fwd_sem.at[k], src).wait_recv()
        copy = remote(out_ref.at[src], src, fwd_sem.at[k], sib)
        copy.start()
        forwards.append(copy)
    remote(out_ref.at[sib], sib, send_sem.at[0], sib).wait_recv()
    for k in range(1, chips):
        src = lax.rem(chip + chips - k, chips) * 2 + 1 - core
        remote(out_ref.at[src], src, fwd_sem.at[k - 1], sib).wait_recv()
    for copy in sends + forwards:
        copy.wait_send()
    local.wait()


def gather_filt(block):
    n = lax.axis_size("filt")
    return pl.pallas_call(
        functools.partial(gather_kernel, n),
        out_shape=jax.ShapeDtypeStruct((n,) + block.shape, block.dtype),
        in_specs=[pl.BlockSpec(memory_space=pl.ANY)],
        out_specs=pl.BlockSpec(memory_space=pl.ANY),
        scratch_shapes=[
            pltpu.SemaphoreType.DMA((1,)),
            pltpu.SemaphoreType.DMA((n // 2,)),
            pltpu.SemaphoreType.DMA((n // 2,)),
            pltpu.SemaphoreType.DMA((n,)),
        ],
        compiler_params=pltpu.CompilerParams(collective_id=0, has_side_effects=True),
    )(block)


def convolve(inputs, weights, padding):
    return lax.conv_general_dilated(
        inputs[None],
        weights,
        (1, 1, 1),
        padding,
        dimension_numbers=("NCDHW", "ODHWI", "NCDHW"),
        preferred_element_type=jnp.float32,
    )[0]


def finish(summed, filter_bias):
    activated = summed + filter_bias.astype(jnp.float32)[:, None, None, None]
    activated = jnp.where(activated > 0, activated, slope * activated)
    filters, depth, height, across = activated.shape
    blocked = activated.reshape(filters, depth // 2, 2, height // 2, 2, across // 2, 2)
    return jnp.max(blocked, axis=(2, 4, 6)).astype(jnp.bfloat16)


def on_device(volume, kernel, filter_bias):
    padded = with_halo(volume, (("space", 1),), 1)
    gathered = gather_filt(padded)
    gathered = gathered.reshape((-1,) + gathered.shape[2:])
    summed = convolve(gathered, kernel, ((0, 0), (1, 1), (1, 1)))
    return finish(summed, filter_bias)


def solution(mesh):
    in_specs = (P("filt", "space", None, None), P("filt", None, None, None, None), P("filt"))
    out_specs = P("filt", "space", None, None)
    return jax.shard_map(
        on_device, mesh=mesh, in_specs=in_specs, out_specs=out_specs, check_vma=False
    )
```

```python
import functools

import jax
import jax.numpy as jnp
from jax import lax
from jax.experimental import pallas as pl
from jax.experimental.pallas import tpu as pltpu
from jax.sharding import PartitionSpec as P

slope = 0.3
MESH = pl.DeviceIdType.MESH


def with_halo(block, sides, width):
    for axis, dim in sides:
        count = lax.axis_size(axis)
        forward = [(i, i + 1) for i in range(count - 1)]
        backward = [(target, source) for source, target in forward]
        low = lax.ppermute(
            lax.slice_in_dim(block, block.shape[dim] - width, None, axis=dim), axis, forward
        )
        high = lax.ppermute(lax.slice_in_dim(block, 0, width, axis=dim), axis, backward)
        block = jnp.concatenate([low, block, high], axis=dim)
    return block


def gather_kernel(n, x_ref, out_ref, local_sem, send_sem, fwd_sem, recv_sem):
    me = lax.axis_index("filt")
    sp = lax.axis_index("space")
    chips = n // 2
    core = lax.rem(me, 2)
    chip = me // 2
    sib = me + 1 - 2 * core
    peers = [lax.rem(chip + k, chips) * 2 + core for k in range(1, chips)]
    sources = [lax.rem(chip + chips - k, chips) * 2 + core for k in range(1, chips)]
    rows = x_ref.shape[0]

    def rows_of(slot):
        return pl.ds(pl.multiple_of(slot * rows, rows), rows)

    barrier = pltpu.get_barrier_semaphore()
    for peer in [sib] + peers:
        pl.semaphore_signal(barrier, inc=1, device_id=(peer, sp), device_id_type=MESH)
    pl.semaphore_wait(barrier, chips)

    def remote(src, dst_slot, sem, dev):
        return pltpu.make_async_remote_copy(
            src_ref=src,
            dst_ref=out_ref.at[rows_of(dst_slot)],
            send_sem=sem,
            recv_sem=recv_sem.at[dst_slot],
            device_id=(dev, sp),
            device_id_type=MESH,
        )

    local = pltpu.make_async_copy(x_ref, out_ref.at[rows_of(me)], local_sem.at[0])
    local.start()
    sends = [remote(x_ref, me, send_sem.at[0], sib)]
    for k, peer in enumerate(peers):
        sends.append(remote(x_ref, me, send_sem.at[k + 1], peer))
    for copy in sends:
        copy.start()
    forwards = []
    for k, src in enumerate(sources):
        remote(out_ref.at[rows_of(src)], src, fwd_sem.at[k], src).wait_recv()
        copy = remote(out_ref.at[rows_of(src)], src, fwd_sem.at[k], sib)
        copy.start()
        forwards.append(copy)
    remote(out_ref.at[rows_of(sib)], sib, send_sem.at[0], sib).wait_recv()
    for k in range(1, chips):
        src = lax.rem(chip + chips - k, chips) * 2 + 1 - core
        remote(out_ref.at[rows_of(src)], src, fwd_sem.at[k - 1], sib).wait_recv()
    for copy in sends + forwards:
        copy.wait_send()
    local.wait()


def gather_filt(block):
    n = lax.axis_size("filt")
    return pl.pallas_call(
        functools.partial(gather_kernel, n),
        out_shape=jax.ShapeDtypeStruct((n * block.shape[0],) + block.shape[1:], block.dtype),
        in_specs=[pl.BlockSpec(memory_space=pl.ANY)],
        out_specs=pl.BlockSpec(memory_space=pl.ANY),
        scratch_shapes=[
            pltpu.SemaphoreType.DMA((1,)),
            pltpu.SemaphoreType.DMA((n // 2,)),
            pltpu.SemaphoreType.DMA((n // 2,)),
            pltpu.SemaphoreType.DMA((n,)),
        ],
        compiler_params=pltpu.CompilerParams(collective_id=0, has_side_effects=True),
    )(block)


def conv_kernel(g_ref, w_ref, b_ref, o_ref, *, plane, row, depth):
    g = g_ref[...]
    cols = g.shape[1]
    x = lax.broadcasted_iota(jnp.int32, g.shape, 1) % row
    zero = jnp.zeros_like(g)
    left = jnp.where(x == 0, zero, pltpu.roll(g, 1, 1))
    right = jnp.where(x == row - 1, zero, pltpu.roll(g, cols - 1, 1))
    stacked = jnp.concatenate([left, g, right], axis=0)
    q = jnp.dot(w_ref[...], stacked, preferred_element_type=jnp.float32)
    filters = o_ref.shape[0]
    out_cols = depth * plane
    acc = jnp.zeros((filters, out_cols), jnp.float32)
    for a in range(3):
        for b in range(3):
            tap = q[(a * 3 + b) * filters:(a * 3 + b + 1) * filters]
            shift = a * plane + (b - 1) * row
            if b == 1:
                acc = acc + tap[:, shift:shift + out_cols]
                continue
            pieces = []
            for z in range(depth):
                lo = z * plane + (row if b == 0 else 0)
                hi = lo + plane - row
                part = tap[:, lo + shift:hi + shift]
                edge = jnp.zeros((filters, row), jnp.float32)
                pieces += [edge, part] if b == 0 else [part, edge]
            acc = acc + jnp.concatenate(pieces, axis=1)
    pooled = []
    for zp in range(depth // 2):
        zmax = jnp.maximum(
            acc[:, 2 * zp * plane:(2 * zp + 1) * plane],
            acc[:, (2 * zp + 1) * plane:(2 * zp + 2) * plane],
        )
        for yp in range(plane // row // 2):
            pooled.append(
                jnp.maximum(
                    zmax[:, 2 * yp * row:(2 * yp + 1) * row],
                    zmax[:, (2 * yp + 1) * row:(2 * yp + 2) * row],
                )
            )
    m = jnp.concatenate(pooled, axis=1)
    m = jnp.maximum(m, pltpu.roll(m, m.shape[1] - 1, 1))
    v = m + b_ref[...]
    v = jnp.where(v > 0, v, slope * v).astype(jnp.bfloat16)
    r = lax.broadcasted_iota(jnp.int32, (m.shape[1], m.shape[1] // 2), 0)
    c = lax.broadcasted_iota(jnp.int32, (m.shape[1], m.shape[1] // 2), 1)
    pick = (r == 2 * c).astype(jnp.bfloat16)
    o_ref[...] = jnp.dot(v, pick, preferred_element_type=jnp.float32).astype(o_ref.dtype)


def conv_pool(gathered, kernel, filter_bias, depth, height, across):
    filters = kernel.shape[0]
    weights = kernel.transpose(1, 2, 0, 3, 4).reshape(9 * filters, -1)
    bias = filter_bias.astype(jnp.float32).reshape(filters, 1)
    plane = height * across
    out = pl.pallas_call(
        functools.partial(conv_kernel, plane=plane, row=across, depth=depth),
        out_shape=jax.ShapeDtypeStruct((filters, depth * plane // 8), jnp.bfloat16),
        in_specs=[pl.BlockSpec(memory_space=pltpu.VMEM)] * 3,
        out_specs=pl.BlockSpec(memory_space=pltpu.VMEM),
    )(gathered, weights, bias)
    return out.reshape(filters, depth // 2, height // 2, across // 2)


def on_device(volume, kernel, filter_bias):
    local_in, depth, height, across = volume.shape
    padded = with_halo(volume, (("space", 1),), 1)
    gathered = gather_filt(padded.reshape(local_in, -1))
    return conv_pool(gathered, kernel, filter_bias, depth, height, across)


def solution(mesh):
    in_specs = (P("filt", "space", None, None), P("filt", None, None, None, None), P("filt"))
    out_specs = P("filt", "space", None, None)
    return jax.shard_map(
        on_device, mesh=mesh, in_specs=in_specs, out_specs=out_specs, check_vma=False
    )
```

```python
import functools

import jax
import jax.numpy as jnp
from jax import lax
from jax.experimental import pallas as pl
from jax.experimental.pallas import tpu as pltpu
from jax.sharding import PartitionSpec as P

slope = 0.3
MESH = pl.DeviceIdType.MESH


def gather_kernel(n, slabs, x_ref, out_ref, local_sem, send_sem, fwd_sem, halo_sem,
                  recv_sem, lo_sem, hi_sem):
    me = lax.axis_index("filt")
    sp = lax.axis_index("space")
    chips = n // 2
    core = lax.rem(me, 2)
    chip = me // 2
    sib = me + 1 - 2 * core
    peers = [lax.rem(chip + k, chips) * 2 + core for k in range(1, chips)]
    sources = [lax.rem(chip + chips - k, chips) * 2 + core for k in range(1, chips)]
    rows, cols = x_ref.shape
    plane = cols // 4
    has_lo = sp > 0
    has_hi = sp < slabs - 1

    def rows_of(slot):
        return pl.ds(pl.multiple_of(slot * rows, rows), rows)

    def main_at(slot):
        return out_ref.at[rows_of(slot), pl.ds(plane, cols)]

    def lo_at(slot):
        return out_ref.at[rows_of(slot), pl.ds(0, plane)]

    def hi_at(slot):
        return out_ref.at[rows_of(slot), pl.ds(plane + cols, plane)]

    barrier = pltpu.get_barrier_semaphore()
    for peer in [sib] + peers:
        pl.semaphore_signal(barrier, inc=1, device_id=(peer, sp), device_id_type=MESH)

    @pl.when(has_lo)
    def _():
        pl.semaphore_signal(barrier, inc=1, device_id=(me, sp - 1), device_id_type=MESH)

    @pl.when(has_hi)
    def _():
        pl.semaphore_signal(barrier, inc=1, device_id=(me, sp + 1), device_id_type=MESH)

    pl.semaphore_wait(barrier, chips + has_lo.astype(jnp.int32) + has_hi.astype(jnp.int32))

    def copy(src, dst, sem, recv, dev):
        return pltpu.make_async_remote_copy(
            src_ref=src, dst_ref=dst, send_sem=sem, recv_sem=recv,
            device_id=dev, device_id_type=MESH,
        )

    def main_copy(src, slot, sem, dev):
        return copy(src, main_at(slot), sem, recv_sem.at[slot], (dev, sp))

    def halo_out(src_rows, slot, k):
        down = copy(src_rows(0), hi_at(slot), halo_sem.at[0, k], hi_sem.at[slot], (me, sp - 1))
        up = copy(src_rows(3), lo_at(slot), halo_sem.at[1, k], lo_sem.at[slot], (me, sp + 1))

        @pl.when(has_lo)
        def _():
            down.start()

        @pl.when(has_hi)
        def _():
            up.start()

        return down, up

    local = pltpu.make_async_copy(x_ref, main_at(me), local_sem.at[0])
    local.start()
    sends = [main_copy(x_ref, me, send_sem.at[0], sib)]
    for k, peer in enumerate(peers):
        sends.append(main_copy(x_ref, me, send_sem.at[k + 1], peer))
    for c in sends:
        c.start()
    halos = [halo_out(lambda p: x_ref.at[:, pl.ds(p * plane, plane)], me, 0)]
    forwards = []
    for k, src in enumerate(sources):
        main_copy(main_at(src), src, fwd_sem.at[0, k], src).wait_recv()
        c = main_copy(main_at(src), src, fwd_sem.at[0, k], sib)
        c.start()
        forwards.append(c)
        held = lambda p, src=src: out_ref.at[rows_of(src), pl.ds((p + 1) * plane, plane)]
        halos.append(halo_out(held, src, k + 1))
    same_core = [me] + sources
    lo_fwd, hi_fwd = [], []
    for k, src in enumerate(same_core):
        lo = copy(lo_at(src), lo_at(src), fwd_sem.at[1, k], lo_sem.at[src], (sib, sp))
        hi = copy(hi_at(src), hi_at(src), fwd_sem.at[2, k], hi_sem.at[src], (sib, sp))

        @pl.when(has_lo)
        def _():
            lo.wait_recv()
            lo.start()

        @pl.when(has_hi)
        def _():
            hi.wait_recv()
            hi.start()

        lo_fwd.append(lo)
        hi_fwd.append(hi)
    main_copy(main_at(sib), sib, send_sem.at[0], sib).wait_recv()
    for k in range(1, chips):
        src = lax.rem(chip + chips - k, chips) * 2 + 1 - core
        main_copy(main_at(src), src, fwd_sem.at[0, k - 1], sib).wait_recv()
    other_core = [sib] + [lax.rem(chip + chips - k, chips) * 2 + 1 - core for k in range(1, chips)]
    for k, src in enumerate(other_core):
        lo = copy(lo_at(src), lo_at(src), fwd_sem.at[1, k], lo_sem.at[src], (sib, sp))
        hi = copy(hi_at(src), hi_at(src), fwd_sem.at[2, k], hi_sem.at[src], (sib, sp))

        @pl.when(has_lo)
        def _():
            lo.wait_recv()

        @pl.when(has_hi)
        def _():
            hi.wait_recv()

    for c in sends + forwards:
        c.wait_send()
    for down, up in halos:
        @pl.when(has_lo)
        def _():
            down.wait_send()

        @pl.when(has_hi)
        def _():
            up.wait_send()

    for lo, hi in zip(lo_fwd, hi_fwd):
        @pl.when(has_lo)
        def _():
            lo.wait_send()

        @pl.when(has_hi)
        def _():
            hi.wait_send()

    local.wait()


def gather_filt(block):
    n = lax.axis_size("filt")
    slabs = lax.axis_size("space")
    rows, cols = block.shape
    chips = n // 2
    return pl.pallas_call(
        functools.partial(gather_kernel, n, slabs),
        out_shape=jax.ShapeDtypeStruct((n * rows, cols + cols // 2), block.dtype),
        in_specs=[pl.BlockSpec(memory_space=pl.ANY)],
        out_specs=pl.BlockSpec(memory_space=pl.ANY),
        scratch_shapes=[
            pltpu.SemaphoreType.DMA((1,)),
            pltpu.SemaphoreType.DMA((chips,)),
            pltpu.SemaphoreType.DMA((3, chips)),
            pltpu.SemaphoreType.DMA((2, chips)),
            pltpu.SemaphoreType.DMA((n,)),
            pltpu.SemaphoreType.DMA((n,)),
            pltpu.SemaphoreType.DMA((n,)),
        ],
        compiler_params=pltpu.CompilerParams(collective_id=0, has_side_effects=True),
    )(block)


def conv_kernel(g_ref, w_ref, b_ref, o_ref, *, plane, row, depth, slabs):
    sp = lax.axis_index("space")
    g = g_ref[...]
    cols = g.shape[1]
    col = lax.broadcasted_iota(jnp.int32, g.shape, 1)
    zero = jnp.zeros_like(g)
    edge = ((col < plane) & (sp == 0)) | ((col >= cols - plane) & (sp == slabs - 1))
    g = jnp.where(edge, zero, g)
    x = col % row
    left = jnp.where(x == 0, zero, pltpu.roll(g, 1, 1))
    right = jnp.where(x == row - 1, zero, pltpu.roll(g, cols - 1, 1))
    stacked = jnp.concatenate([left, g, right], axis=0)
    weights = jnp.concatenate(
        [jnp.concatenate([w_ref[a, b, c] for c in range(3)], axis=1)
         for a in range(3) for b in range(3)],
        axis=0,
    )
    q = jnp.dot(weights, stacked, preferred_element_type=jnp.float32)
    filters = w_ref.shape[3]
    out_cols = depth * plane
    acc = jnp.zeros((filters, out_cols), jnp.float32)
    for a in range(3):
        for b in range(3):
            tap = q[(a * 3 + b) * filters:(a * 3 + b + 1) * filters]
            shift = a * plane + (b - 1) * row
            if b == 1:
                acc = acc + tap[:, shift:shift + out_cols]
                continue
            pieces = []
            for z in range(depth):
                lo = z * plane + (row if b == 0 else 0)
                hi = lo + plane - row
                part = tap[:, lo + shift:hi + shift]
                pad = jnp.zeros((filters, row), jnp.float32)
                pieces += [pad, part] if b == 0 else [part, pad]
            acc = acc + jnp.concatenate(pieces, axis=1)
    pooled = []
    for zp in range(depth // 2):
        zmax = jnp.maximum(
            acc[:, 2 * zp * plane:(2 * zp + 1) * plane],
            acc[:, (2 * zp + 1) * plane:(2 * zp + 2) * plane],
        )
        for yp in range(plane // row // 2):
            pooled.append(
                jnp.maximum(
                    zmax[:, 2 * yp * row:(2 * yp + 1) * row],
                    zmax[:, (2 * yp + 1) * row:(2 * yp + 2) * row],
                )
            )
    m = jnp.concatenate(pooled, axis=1)
    m = jnp.maximum(m, pltpu.roll(m, m.shape[1] - 1, 1))
    brow = jnp.broadcast_to(b_ref[...].astype(jnp.float32), (filters, filters))
    r16 = lax.broadcasted_iota(jnp.int32, (filters, filters), 0)
    c16 = lax.broadcasted_iota(jnp.int32, (filters, filters), 1)
    bias = jnp.sum(jnp.where(r16 == c16, brow, 0.0), axis=1, keepdims=True)
    v = m + bias
    v = jnp.where(v > 0, v, slope * v).astype(jnp.bfloat16)
    r = lax.broadcasted_iota(jnp.int32, (m.shape[1], m.shape[1] // 2), 0)
    c = lax.broadcasted_iota(jnp.int32, (m.shape[1], m.shape[1] // 2), 1)
    pick = (r == 2 * c).astype(jnp.bfloat16)
    o_ref[...] = jnp.dot(v, pick, preferred_element_type=jnp.float32).astype(o_ref.dtype)


def conv_pool(gathered, kernel, filter_bias, depth, height, across):
    filters = kernel.shape[0]
    weights = kernel.transpose(1, 2, 3, 0, 4)
    bias = filter_bias.reshape(1, filters)
    plane = height * across
    out = pl.pallas_call(
        functools.partial(conv_kernel, plane=plane, row=across, depth=depth,
                          slabs=lax.axis_size("space")),
        out_shape=jax.ShapeDtypeStruct((filters, depth * plane // 8), jnp.bfloat16),
        in_specs=[pl.BlockSpec(memory_space=pltpu.VMEM)] * 3,
        out_specs=pl.BlockSpec(memory_space=pltpu.VMEM),
    )(gathered, weights, bias)
    return out.reshape(filters, depth // 2, height // 2, across // 2)


def on_device(volume, kernel, filter_bias):
    local_in, depth, height, across = volume.shape
    gathered = gather_filt(volume.reshape(local_in, -1))
    return conv_pool(gathered, kernel, filter_bias, depth, height, across)


def solution(mesh):
    in_specs = (P("filt", "space", None, None), P("filt", None, None, None, None), P("filt"))
    out_specs = P("filt", "space", None, None)
    return jax.shard_map(
        on_device, mesh=mesh, in_specs=in_specs, out_specs=out_specs, check_vma=False
    )
```

```python
import functools

import jax
import jax.numpy as jnp
from jax import lax
from jax.experimental import pallas as pl
from jax.experimental.pallas import tpu as pltpu
from jax.sharding import PartitionSpec as P

slope = 0.3
MESH = pl.DeviceIdType.MESH


def gather_kernel(n, slabs, v_ref, out_ref, x_ref, local_sem, send_sem, fwd_sem, halo_sem,
                  recv_sem, lo_sem, hi_sem):
    depth, height = v_ref.shape[1], v_ref.shape[2]
    across = v_ref.shape[3]
    for z in range(depth):
        for y in range(height):
            x_ref[:, pl.ds((z * height + y) * across, across)] = v_ref[:, z, y, :]
    me = lax.axis_index("filt")
    sp = lax.axis_index("space")
    chips = n // 2
    core = lax.rem(me, 2)
    chip = me // 2
    sib = me + 1 - 2 * core
    peers = [lax.rem(chip + k, chips) * 2 + core for k in range(1, chips)]
    sources = [lax.rem(chip + chips - k, chips) * 2 + core for k in range(1, chips)]
    rows, cols = x_ref.shape
    plane = cols // 4
    has_lo = sp > 0
    has_hi = sp < slabs - 1

    def rows_of(slot):
        return pl.ds(pl.multiple_of(slot * rows, rows), rows)

    def main_at(slot):
        return out_ref.at[rows_of(slot), pl.ds(plane, cols)]

    def lo_at(slot):
        return out_ref.at[rows_of(slot), pl.ds(0, plane)]

    def hi_at(slot):
        return out_ref.at[rows_of(slot), pl.ds(plane + cols, plane)]

    barrier = pltpu.get_barrier_semaphore()
    for peer in [sib] + peers:
        pl.semaphore_signal(barrier, inc=1, device_id=(peer, sp), device_id_type=MESH)

    @pl.when(has_lo)
    def _():
        pl.semaphore_signal(barrier, inc=1, device_id=(me, sp - 1), device_id_type=MESH)

    @pl.when(has_hi)
    def _():
        pl.semaphore_signal(barrier, inc=1, device_id=(me, sp + 1), device_id_type=MESH)

    pl.semaphore_wait(barrier, chips + has_lo.astype(jnp.int32) + has_hi.astype(jnp.int32))

    def copy(src, dst, sem, recv, dev):
        return pltpu.make_async_remote_copy(
            src_ref=src, dst_ref=dst, send_sem=sem, recv_sem=recv,
            device_id=dev, device_id_type=MESH,
        )

    def main_copy(src, slot, sem, dev):
        return copy(src, main_at(slot), sem, recv_sem.at[slot], (dev, sp))

    def halo_out(src_rows, slot, k):
        down = copy(src_rows(0), hi_at(slot), halo_sem.at[0, k], hi_sem.at[slot], (me, sp - 1))
        up = copy(src_rows(3), lo_at(slot), halo_sem.at[1, k], lo_sem.at[slot], (me, sp + 1))

        @pl.when(has_lo)
        def _():
            down.start()

        @pl.when(has_hi)
        def _():
            up.start()

        return down, up

    local = pltpu.make_async_copy(x_ref, main_at(me), local_sem.at[0])
    local.start()
    sends = [main_copy(x_ref, me, send_sem.at[0], sib)]
    for k, peer in enumerate(peers):
        sends.append(main_copy(x_ref, me, send_sem.at[k + 1], peer))
    for c in sends:
        c.start()
    halos = [halo_out(lambda p: x_ref.at[:, pl.ds(p * plane, plane)], me, 0)]
    forwards = []
    for k, src in enumerate(sources):
        main_copy(main_at(src), src, fwd_sem.at[0, k], src).wait_recv()
        c = main_copy(main_at(src), src, fwd_sem.at[0, k], sib)
        c.start()
        forwards.append(c)
        held = lambda p, src=src: out_ref.at[rows_of(src), pl.ds((p + 1) * plane, plane)]
        halos.append(halo_out(held, src, k + 1))
    same_core = [me] + sources
    lo_fwd, hi_fwd = [], []
    for k, src in enumerate(same_core):
        lo = copy(lo_at(src), lo_at(src), fwd_sem.at[1, k], lo_sem.at[src], (sib, sp))
        hi = copy(hi_at(src), hi_at(src), fwd_sem.at[2, k], hi_sem.at[src], (sib, sp))

        @pl.when(has_lo)
        def _():
            lo.wait_recv()
            lo.start()

        @pl.when(has_hi)
        def _():
            hi.wait_recv()
            hi.start()

        lo_fwd.append(lo)
        hi_fwd.append(hi)
    main_copy(main_at(sib), sib, send_sem.at[0], sib).wait_recv()
    for k in range(1, chips):
        src = lax.rem(chip + chips - k, chips) * 2 + 1 - core
        main_copy(main_at(src), src, fwd_sem.at[0, k - 1], sib).wait_recv()
    other_core = [sib] + [lax.rem(chip + chips - k, chips) * 2 + 1 - core for k in range(1, chips)]
    for k, src in enumerate(other_core):
        lo = copy(lo_at(src), lo_at(src), fwd_sem.at[1, k], lo_sem.at[src], (sib, sp))
        hi = copy(hi_at(src), hi_at(src), fwd_sem.at[2, k], hi_sem.at[src], (sib, sp))

        @pl.when(has_lo)
        def _():
            lo.wait_recv()

        @pl.when(has_hi)
        def _():
            hi.wait_recv()

    for c in sends + forwards:
        c.wait_send()
    for down, up in halos:
        @pl.when(has_lo)
        def _():
            down.wait_send()

        @pl.when(has_hi)
        def _():
            up.wait_send()

    for lo, hi in zip(lo_fwd, hi_fwd):
        @pl.when(has_lo)
        def _():
            lo.wait_send()

        @pl.when(has_hi)
        def _():
            hi.wait_send()

    local.wait()


def gather_filt(block):
    n = lax.axis_size("filt")
    slabs = lax.axis_size("space")
    rows = block.shape[0]
    cols = block.size // rows
    chips = n // 2
    return pl.pallas_call(
        functools.partial(gather_kernel, n, slabs),
        out_shape=jax.ShapeDtypeStruct((n * rows, cols + cols // 2), block.dtype),
        in_specs=[pl.BlockSpec(memory_space=pltpu.VMEM)],
        out_specs=pl.BlockSpec(memory_space=pl.ANY),
        scratch_shapes=[
            pltpu.VMEM((rows, cols), block.dtype),
            pltpu.SemaphoreType.DMA((1,)),
            pltpu.SemaphoreType.DMA((chips,)),
            pltpu.SemaphoreType.DMA((3, chips)),
            pltpu.SemaphoreType.DMA((2, chips)),
            pltpu.SemaphoreType.DMA((n,)),
            pltpu.SemaphoreType.DMA((n,)),
            pltpu.SemaphoreType.DMA((n,)),
        ],
        compiler_params=pltpu.CompilerParams(collective_id=0, has_side_effects=True),
    )(block)


def conv_kernel(g_ref, w_ref, b_ref, o_ref, *, plane, row, depth, slabs):
    sp = lax.axis_index("space")
    g = g_ref[...]
    cols = g.shape[1]
    col = lax.broadcasted_iota(jnp.int32, g.shape, 1)
    zero = jnp.zeros_like(g)
    edge = ((col < plane) & (sp == 0)) | ((col >= cols - plane) & (sp == slabs - 1))
    g = jnp.where(edge, zero, g)
    x = col % row
    left = jnp.where(x == 0, zero, pltpu.roll(g, 1, 1))
    right = jnp.where(x == row - 1, zero, pltpu.roll(g, cols - 1, 1))
    stacked = jnp.concatenate([left, g, right], axis=0)
    weights = jnp.concatenate(
        [jnp.concatenate([w_ref[a, b, c] for c in range(3)], axis=1)
         for a in range(3) for b in range(3)],
        axis=0,
    )
    q = jnp.dot(weights, stacked, preferred_element_type=jnp.float32)
    filters = w_ref.shape[3]
    out_cols = depth * plane
    acc = jnp.zeros((filters, out_cols), jnp.float32)
    for a in range(3):
        for b in range(3):
            tap = q[(a * 3 + b) * filters:(a * 3 + b + 1) * filters]
            shift = a * plane + (b - 1) * row
            if b == 1:
                acc = acc + tap[:, shift:shift + out_cols]
                continue
            pieces = []
            for z in range(depth):
                lo = z * plane + (row if b == 0 else 0)
                hi = lo + plane - row
                part = tap[:, lo + shift:hi + shift]
                pad = jnp.zeros((filters, row), jnp.float32)
                pieces += [pad, part] if b == 0 else [part, pad]
            acc = acc + jnp.concatenate(pieces, axis=1)
    pooled = []
    for zp in range(depth // 2):
        zmax = jnp.maximum(
            acc[:, 2 * zp * plane:(2 * zp + 1) * plane],
            acc[:, (2 * zp + 1) * plane:(2 * zp + 2) * plane],
        )
        for yp in range(plane // row // 2):
            pooled.append(
                jnp.maximum(
                    zmax[:, 2 * yp * row:(2 * yp + 1) * row],
                    zmax[:, (2 * yp + 1) * row:(2 * yp + 2) * row],
                )
            )
    m = jnp.concatenate(pooled, axis=1)
    m = jnp.maximum(m, pltpu.roll(m, m.shape[1] - 1, 1))
    brow = jnp.broadcast_to(b_ref[...].astype(jnp.float32), (filters, filters))
    r16 = lax.broadcasted_iota(jnp.int32, (filters, filters), 0)
    c16 = lax.broadcasted_iota(jnp.int32, (filters, filters), 1)
    bias = jnp.sum(jnp.where(r16 == c16, brow, 0.0), axis=1, keepdims=True)
    v = m + bias
    v = jnp.where(v > 0, v, slope * v).astype(jnp.bfloat16)
    r = lax.broadcasted_iota(jnp.int32, (m.shape[1], m.shape[1] // 2), 0)
    c = lax.broadcasted_iota(jnp.int32, (m.shape[1], m.shape[1] // 2), 1)
    pick = (r == 2 * c).astype(jnp.bfloat16)
    picked = jnp.dot(v, pick, preferred_element_type=jnp.float32).astype(o_ref.dtype)
    half = row // 2
    for zp in range(o_ref.shape[1]):
        for yp in range(o_ref.shape[2]):
            k = zp * o_ref.shape[2] + yp
            o_ref[:, zp, yp, :] = picked[:, k * half:(k + 1) * half]


def conv_pool(gathered, kernel, filter_bias, depth, height, across):
    filters = kernel.shape[0]
    weights = kernel.transpose(1, 2, 3, 0, 4)
    bias = filter_bias.reshape(1, filters)
    plane = height * across
    out = pl.pallas_call(
        functools.partial(conv_kernel, plane=plane, row=across, depth=depth,
                          slabs=lax.axis_size("space")),
        out_shape=jax.ShapeDtypeStruct((filters, depth // 2, height // 2, across // 2), jnp.bfloat16),
        in_specs=[pl.BlockSpec(memory_space=pltpu.VMEM)] * 3,
        out_specs=pl.BlockSpec(memory_space=pltpu.VMEM),
    )(gathered, weights, bias)
    return out


def on_device(volume, kernel, filter_bias):
    local_in, depth, height, across = volume.shape
    gathered = gather_filt(volume)
    return conv_pool(gathered, kernel, filter_bias, depth, height, across)


def solution(mesh):
    in_specs = (P("filt", "space", None, None), P("filt", None, None, None, None), P("filt"))
    out_specs = P("filt", "space", None, None)
    return jax.shard_map(
        on_device, mesh=mesh, in_specs=in_specs, out_specs=out_specs, check_vma=False
    )
```

```python
import functools

import jax
import jax.numpy as jnp
from jax import lax
from jax.experimental import pallas as pl
from jax.experimental.pallas import tpu as pltpu
from jax.sharding import PartitionSpec as P

slope = 0.3
MESH = pl.DeviceIdType.MESH


def gather_kernel(n, slabs, v_ref, out_ref, x_ref, local_sem, send_sem, fwd_sem, relay_sem,
                  halo_sem, recv_sem, lo_sem, hi_sem):
    depth, height, across = v_ref.shape[1:]
    for z in range(depth):
        for y in range(height):
            x_ref[:, pl.ds((z * height + y) * across, across)] = v_ref[:, z, y, :]
    me = lax.axis_index("filt")
    sp = lax.axis_index("space")
    chips = n // 2
    zn = 4
    yn = chips // zn
    core = lax.rem(me, 2)
    chip = me // 2
    yy, zz = chip // zn, lax.rem(chip, zn)
    sib = me + 1 - 2 * core

    def dev(dy, dz):
        return (lax.rem(yy + dy + yn, yn) * zn + lax.rem(zz + dz + zn, zn)) * 2 + core

    direct = [(dy, dz) for dz in (1, 3, 0) for dy in range(yn) if (dy, dz) != (0, 0)]
    far = [(dy, 2) for dy in range(yn)]
    peers = [dev(dy, dz) for dy, dz in direct]
    rows, cols = x_ref.shape
    plane = cols // depth
    half = cols // 2
    has_lo = sp > 0
    has_hi = sp < slabs - 1

    def rows_of(slot):
        return pl.ds(pl.multiple_of(slot * rows, rows), rows)

    def main_at(slot):
        return out_ref.at[rows_of(slot), pl.ds(plane, cols)]

    def lo_at(slot):
        return out_ref.at[rows_of(slot), pl.ds(0, plane)]

    def hi_at(slot):
        return out_ref.at[rows_of(slot), pl.ds(plane + cols, plane)]

    barrier = pltpu.get_barrier_semaphore()
    for peer in [sib] + peers:
        pl.semaphore_signal(barrier, inc=1, device_id=(peer, sp), device_id_type=MESH)

    @pl.when(has_lo)
    def _():
        pl.semaphore_signal(barrier, inc=1, device_id=(me, sp - 1), device_id_type=MESH)

    @pl.when(has_hi)
    def _():
        pl.semaphore_signal(barrier, inc=1, device_id=(me, sp + 1), device_id_type=MESH)

    pl.semaphore_wait(
        barrier, 1 + len(peers) + has_lo.astype(jnp.int32) + has_hi.astype(jnp.int32)
    )

    def copy(src, dst, sem, recv, dev_id):
        return pltpu.make_async_remote_copy(
            src_ref=src, dst_ref=dst, send_sem=sem, recv_sem=recv,
            device_id=dev_id, device_id_type=MESH,
        )

    def main_copy(src, slot, sem, dev_id):
        return copy(src, main_at(slot), sem, recv_sem.at[slot], (dev_id, sp))

    def halo_out(src_rows, slot, k):
        down = copy(src_rows(0), hi_at(slot), halo_sem.at[0, k], hi_sem.at[slot], (me, sp - 1))
        up = copy(src_rows(depth - 1), lo_at(slot), halo_sem.at[1, k], lo_sem.at[slot],
                  (me, sp + 1))

        @pl.when(has_lo)
        def _():
            down.start()

        @pl.when(has_hi)
        def _():
            up.start()

        return down, up

    local = pltpu.make_async_copy(x_ref, main_at(me), local_sem.at[0])
    local.start()
    sends = [main_copy(x_ref, me, send_sem.at[0], sib)]
    for k, peer in enumerate(peers):
        sends.append(main_copy(x_ref, me, send_sem.at[k + 1], peer))
    for c in sends:
        c.start()
    halos = [halo_out(lambda p: x_ref.at[:, pl.ds(p * plane, plane)], me, 0)]
    forwards = []
    relays = []
    sources = []
    for k, (dy, dz) in enumerate(direct + far):
        src = dev(-dy, -dz)
        sources.append(src)
        main_copy(main_at(src), src, fwd_sem.at[0, k], src).wait_recv()
        if dz in (1, 3):
            part = pl.ds(plane + (0 if dz == 1 else half), half)
            held = out_ref.at[rows_of(src), part]
            target = dev(0, 1 if dz == 1 else -1)
            r = copy(held, held, relay_sem.at[dz // 2, dy], recv_sem.at[src], (target, sp))
            r.start()
            relays.append(r)
        c = main_copy(main_at(src), src, fwd_sem.at[0, k], sib)
        c.start()
        forwards.append(c)
        held_plane = lambda p, src=src: out_ref.at[rows_of(src), pl.ds((p + 1) * plane, plane)]
        halos.append(halo_out(held_plane, src, k + 1))
    same_core = [me] + sources
    lo_fwd, hi_fwd = [], []
    for k, src in enumerate(same_core):
        lo = copy(lo_at(src), lo_at(src), fwd_sem.at[1, k], lo_sem.at[src], (sib, sp))
        hi = copy(hi_at(src), hi_at(src), fwd_sem.at[2, k], hi_sem.at[src], (sib, sp))

        @pl.when(has_lo)
        def _():
            lo.wait_recv()
            lo.start()

        @pl.when(has_hi)
        def _():
            hi.wait_recv()
            hi.start()

        lo_fwd.append(lo)
        hi_fwd.append(hi)
    other_core = [s + 1 - 2 * core for s in same_core]
    for k, src in enumerate(other_core):
        main_copy(main_at(src), src, fwd_sem.at[0, 0], sib).wait_recv()
        lo = copy(lo_at(src), lo_at(src), fwd_sem.at[1, k], lo_sem.at[src], (sib, sp))
        hi = copy(hi_at(src), hi_at(src), fwd_sem.at[2, k], hi_sem.at[src], (sib, sp))

        @pl.when(has_lo)
        def _():
            lo.wait_recv()

        @pl.when(has_hi)
        def _():
            hi.wait_recv()

    for c in sends + forwards + relays:
        c.wait_send()
    for down, up in halos:
        @pl.when(has_lo)
        def _():
            down.wait_send()

        @pl.when(has_hi)
        def _():
            up.wait_send()

    for lo, hi in zip(lo_fwd, hi_fwd):
        @pl.when(has_lo)
        def _():
            lo.wait_send()

        @pl.when(has_hi)
        def _():
            hi.wait_send()

    local.wait()


def gather_filt(block):
    n = lax.axis_size("filt")
    slabs = lax.axis_size("space")
    rows = block.shape[0]
    cols = block.size // rows
    chips = n // 2
    return pl.pallas_call(
        functools.partial(gather_kernel, n, slabs),
        out_shape=jax.ShapeDtypeStruct((n * rows, cols + cols // 2), block.dtype),
        in_specs=[pl.BlockSpec(memory_space=pltpu.VMEM)],
        out_specs=pl.BlockSpec(memory_space=pl.ANY),
        scratch_shapes=[
            pltpu.VMEM((rows, cols), block.dtype),
            pltpu.SemaphoreType.DMA((1,)),
            pltpu.SemaphoreType.DMA((chips,)),
            pltpu.SemaphoreType.DMA((3, chips)),
            pltpu.SemaphoreType.DMA((2, chips // 4)),
            pltpu.SemaphoreType.DMA((2, chips)),
            pltpu.SemaphoreType.DMA((n,)),
            pltpu.SemaphoreType.DMA((n,)),
            pltpu.SemaphoreType.DMA((n,)),
        ],
        compiler_params=pltpu.CompilerParams(collective_id=0, has_side_effects=True),
    )(block)


def conv_kernel(g_ref, w_ref, b_ref, o_ref, *, plane, row, depth, slabs):
    sp = lax.axis_index("space")
    g = g_ref[...]
    cols = g.shape[1]
    col = lax.broadcasted_iota(jnp.int32, g.shape, 1)
    zero = jnp.zeros_like(g)
    edge = ((col < plane) & (sp == 0)) | ((col >= cols - plane) & (sp == slabs - 1))
    g = jnp.where(edge, zero, g)
    x = col % row
    left = jnp.where(x == 0, zero, pltpu.roll(g, 1, 1))
    right = jnp.where(x == row - 1, zero, pltpu.roll(g, cols - 1, 1))
    stacked = jnp.concatenate([left, g, right], axis=0)
    weights = jnp.concatenate(
        [jnp.concatenate([w_ref[a, b, c] for c in range(3)], axis=1)
         for a in range(3) for b in range(3)],
        axis=0,
    )
    q = jnp.dot(weights, stacked, preferred_element_type=jnp.float32)
    filters = w_ref.shape[3]
    out_cols = depth * plane
    acc = jnp.zeros((filters, out_cols), jnp.float32)
    for a in range(3):
        for b in range(3):
            tap = q[(a * 3 + b) * filters:(a * 3 + b + 1) * filters]
            shift = a * plane + (b - 1) * row
            if b == 1:
                acc = acc + tap[:, shift:shift + out_cols]
                continue
            pieces = []
            for z in range(depth):
                lo = z * plane + (row if b == 0 else 0)
                hi = lo + plane - row
                part = tap[:, lo + shift:hi + shift]
                pad = jnp.zeros((filters, row), jnp.float32)
                pieces += [pad, part] if b == 0 else [part, pad]
            acc = acc + jnp.concatenate(pieces, axis=1)
    pooled = []
    for zp in range(depth // 2):
        zmax = jnp.maximum(
            acc[:, 2 * zp * plane:(2 * zp + 1) * plane],
            acc[:, (2 * zp + 1) * plane:(2 * zp + 2) * plane],
        )
        for yp in range(plane // row // 2):
            pooled.append(
                jnp.maximum(
                    zmax[:, 2 * yp * row:(2 * yp + 1) * row],
                    zmax[:, (2 * yp + 1) * row:(2 * yp + 2) * row],
                )
            )
    m = jnp.concatenate(pooled, axis=1)
    m = jnp.maximum(m, pltpu.roll(m, m.shape[1] - 1, 1))
    brow = jnp.broadcast_to(b_ref[...].astype(jnp.float32), (filters, filters))
    r16 = lax.broadcasted_iota(jnp.int32, (filters, filters), 0)
    c16 = lax.broadcasted_iota(jnp.int32, (filters, filters), 1)
    bias = jnp.sum(jnp.where(r16 == c16, brow, 0.0), axis=1, keepdims=True)
    v = m + bias
    v = jnp.where(v > 0, v, slope * v).astype(jnp.bfloat16)
    r = lax.broadcasted_iota(jnp.int32, (m.shape[1], m.shape[1] // 2), 0)
    c = lax.broadcasted_iota(jnp.int32, (m.shape[1], m.shape[1] // 2), 1)
    pick = (r == 2 * c).astype(jnp.bfloat16)
    picked = jnp.dot(v, pick, preferred_element_type=jnp.float32).astype(o_ref.dtype)
    half = row // 2
    for zp in range(o_ref.shape[1]):
        for yp in range(o_ref.shape[2]):
            k = zp * o_ref.shape[2] + yp
            o_ref[:, zp, yp, :] = picked[:, k * half:(k + 1) * half]


def conv_pool(gathered, kernel, filter_bias, depth, height, across):
    filters = kernel.shape[0]
    weights = kernel.transpose(1, 2, 3, 0, 4)
    bias = filter_bias.reshape(1, filters)
    plane = height * across
    out = pl.pallas_call(
        functools.partial(conv_kernel, plane=plane, row=across, depth=depth,
                          slabs=lax.axis_size("space")),
        out_shape=jax.ShapeDtypeStruct((filters, depth // 2, height // 2, across // 2), jnp.bfloat16),
        in_specs=[pl.BlockSpec(memory_space=pltpu.VMEM)] * 3,
        out_specs=pl.BlockSpec(memory_space=pltpu.VMEM),
    )(gathered, weights, bias)
    return out


def on_device(volume, kernel, filter_bias):
    local_in, depth, height, across = volume.shape
    gathered = gather_filt(volume)
    return conv_pool(gathered, kernel, filter_bias, depth, height, across)


def solution(mesh):
    in_specs = (P("filt", "space", None, None), P("filt", None, None, None, None), P("filt"))
    out_specs = P("filt", "space", None, None)
    return jax.shard_map(
        on_device, mesh=mesh, in_specs=in_specs, out_specs=out_specs, check_vma=False
    )
```

```python
import functools

import jax
import jax.numpy as jnp
from jax import lax
from jax.experimental import pallas as pl
from jax.experimental.pallas import tpu as pltpu
from jax.sharding import PartitionSpec as P

slope = 0.3
MESH = pl.DeviceIdType.MESH


def gather_kernel(n, v_ref, out_ref, x_ref, local_sem, send_sem, fwd_sem, relay_sem, recv_sem):
    depth, height, across = v_ref.shape[1:]
    for z in range(depth):
        for y in range(height):
            x_ref[:, pl.ds((z * height + y) * across, across)] = v_ref[:, z, y, :]
    me = lax.axis_index("filt")
    sp = lax.axis_index("space")
    chips = n // 2
    zn = 4
    yn = chips // zn
    core = lax.rem(me, 2)
    chip = me // 2
    yy, zz = chip // zn, lax.rem(chip, zn)
    sib = me + 1 - 2 * core

    def dev(dy, dz):
        return (lax.rem(yy + dy + yn, yn) * zn + lax.rem(zz + dz + zn, zn)) * 2 + core

    direct = [(dy, dz) for dz in (1, 3, 0) for dy in range(yn) if (dy, dz) != (0, 0)]
    far = [(dy, 2) for dy in range(yn)]
    peers = [dev(dy, dz) for dy, dz in direct]
    rows, cols = x_ref.shape
    plane = cols // depth
    half = cols // 2

    def rows_of(slot):
        return pl.ds(pl.multiple_of(slot * rows, rows), rows)

    def main_at(slot):
        return out_ref.at[rows_of(slot)]

    barrier = pltpu.get_barrier_semaphore()
    for peer in [sib] + peers:
        pl.semaphore_signal(barrier, inc=1, device_id=(peer, sp), device_id_type=MESH)
    pl.semaphore_wait(barrier, 1 + len(peers))

    def copy(src, dst, sem, recv, dev_id):
        return pltpu.make_async_remote_copy(
            src_ref=src, dst_ref=dst, send_sem=sem, recv_sem=recv,
            device_id=dev_id, device_id_type=MESH,
        )

    def main_copy(src, slot, sem, dev_id):
        return copy(src, main_at(slot), sem, recv_sem.at[slot], (dev_id, sp))

    local = pltpu.make_async_copy(x_ref, main_at(me), local_sem.at[0])
    local.start()
    sends = [main_copy(x_ref, me, send_sem.at[0], sib)]
    for k, peer in enumerate(peers):
        sends.append(main_copy(x_ref, me, send_sem.at[k + 1], peer))
    for c in sends:
        c.start()
    forwards = []
    relays = []
    sources = []
    for k, (dy, dz) in enumerate(direct + far):
        src = dev(-dy, -dz)
        sources.append(src)
        main_copy(main_at(src), src, fwd_sem.at[0, k], src).wait_recv()
        if dz in (1, 3):
            part = pl.ds(0 if dz == 1 else half, half)
            held = out_ref.at[rows_of(src), part]
            target = dev(0, 1 if dz == 1 else -1)
            r = copy(held, held, relay_sem.at[dz // 2, dy], recv_sem.at[src], (target, sp))
            r.start()
            relays.append(r)
        c = main_copy(main_at(src), src, fwd_sem.at[0, k], sib)
        c.start()
        forwards.append(c)
    for k in range(chips):
        src = (sources[k - 1] if k else me) + 1 - 2 * core
        main_copy(main_at(src), src, fwd_sem.at[0, 0], sib).wait_recv()
    for c in sends + forwards + relays:
        c.wait_send()
    local.wait()


def gather_filt(block):
    n = lax.axis_size("filt")
    rows = block.shape[0]
    cols = block.size // rows
    chips = n // 2
    return pl.pallas_call(
        functools.partial(gather_kernel, n),
        out_shape=jax.ShapeDtypeStruct((n * rows, cols), block.dtype),
        in_specs=[pl.BlockSpec(memory_space=pltpu.VMEM)],
        out_specs=pl.BlockSpec(memory_space=pl.ANY),
        scratch_shapes=[
            pltpu.VMEM((rows, cols), block.dtype),
            pltpu.SemaphoreType.DMA((1,)),
            pltpu.SemaphoreType.DMA((chips,)),
            pltpu.SemaphoreType.DMA((1, chips)),
            pltpu.SemaphoreType.DMA((2, chips // 4)),
            pltpu.SemaphoreType.DMA((n,)),
        ],
        compiler_params=pltpu.CompilerParams(collective_id=0, has_side_effects=True),
    )(block)


def conv_kernel(g_ref, w_ref, b_ref, o_ref, send_buf, recv_buf, send_sem, recv_sem, *,
                plane, row, depth, slabs):
    sp = lax.axis_index("space")
    me = lax.axis_index("filt")
    has_lo = sp > 0
    has_hi = sp < slabs - 1
    g = g_ref[...]
    cols = g.shape[1]
    heights = plane // row
    x = lax.broadcasted_iota(jnp.int32, g.shape, 1) % row
    zero = jnp.zeros_like(g)
    left = jnp.where(x == 0, zero, pltpu.roll(g, 1, 1))
    right = jnp.where(x == row - 1, zero, pltpu.roll(g, cols - 1, 1))
    stacked = jnp.concatenate([left, g, right], axis=0)
    weights = jnp.concatenate(
        [jnp.concatenate([w_ref[a, b, c] for c in range(3)], axis=1)
         for a in range(3) for b in range(3)],
        axis=0,
    )
    q = jnp.dot(weights, stacked, preferred_element_type=jnp.float32)
    filters = w_ref.shape[3]

    def tap_row(a, b, p, y):
        if not 0 <= y < heights:
            return None
        t = (a * 3 + b) * filters
        c0 = p * plane + y * row
        return q[t:t + filters, c0:c0 + row]

    def plane_sum(a, p):
        out = []
        for y in range(heights):
            parts = [tap_row(a, b, p, y + b - 1) for b in range(3)]
            parts = [v for v in parts if v is not None]
            total = parts[0]
            for v in parts[1:]:
                total = total + v
            out.append(total)
        return out

    send_buf[0] = jnp.concatenate(plane_sum(0, depth - 1), axis=1)
    send_buf[1] = jnp.concatenate(plane_sum(2, 0), axis=1)
    barrier = pltpu.get_barrier_semaphore()

    @pl.when(has_lo)
    def _():
        pl.semaphore_signal(barrier, inc=1, device_id=(me, sp - 1), device_id_type=MESH)

    @pl.when(has_hi)
    def _():
        pl.semaphore_signal(barrier, inc=1, device_id=(me, sp + 1), device_id_type=MESH)

    pl.semaphore_wait(barrier, has_lo.astype(jnp.int32) + has_hi.astype(jnp.int32))
    up = pltpu.make_async_remote_copy(
        src_ref=send_buf.at[0], dst_ref=recv_buf.at[0], send_sem=send_sem.at[0],
        recv_sem=recv_sem.at[0], device_id=(me, sp + 1), device_id_type=MESH,
    )
    down = pltpu.make_async_remote_copy(
        src_ref=send_buf.at[1], dst_ref=recv_buf.at[1], send_sem=send_sem.at[1],
        recv_sem=recv_sem.at[1], device_id=(me, sp - 1), device_id_type=MESH,
    )

    @pl.when(has_hi)
    def _():
        up.start()

    @pl.when(has_lo)
    def _():
        down.start()

    acc = []
    for z in range(depth):
        rows_z = None
        for a in range(3):
            p = z + a - 1
            if not 0 <= p < depth:
                continue
            part = plane_sum(a, p)
            rows_z = part if rows_z is None else [u + v for u, v in zip(rows_z, part)]
        acc.append(rows_z)

    @pl.when(has_hi)
    def _():
        up.wait_send()
        down_recv = pltpu.make_async_remote_copy(
            src_ref=send_buf.at[1], dst_ref=recv_buf.at[1], send_sem=send_sem.at[1],
            recv_sem=recv_sem.at[1], device_id=(me, sp + 1), device_id_type=MESH,
        )
        down_recv.wait_recv()

    @pl.when(has_lo)
    def _():
        down.wait_send()
        up_recv = pltpu.make_async_remote_copy(
            src_ref=send_buf.at[0], dst_ref=recv_buf.at[0], send_sem=send_sem.at[0],
            recv_sem=recv_sem.at[0], device_id=(me, sp - 1), device_id_type=MESH,
        )
        up_recv.wait_recv()

    below = jnp.where(has_lo, recv_buf[0], 0.0)
    above = jnp.where(has_hi, recv_buf[1], 0.0)
    acc[0] = [v + below[:, y * row:(y + 1) * row] for y, v in enumerate(acc[0])]
    acc[depth - 1] = [v + above[:, y * row:(y + 1) * row] for y, v in enumerate(acc[depth - 1])]
    pooled = []
    for zp in range(depth // 2):
        zmax = [jnp.maximum(u, v) for u, v in zip(acc[2 * zp], acc[2 * zp + 1])]
        for yp in range(heights // 2):
            pooled.append(jnp.maximum(zmax[2 * yp], zmax[2 * yp + 1]))
    m = jnp.concatenate(pooled, axis=1)
    m = jnp.maximum(m, pltpu.roll(m, m.shape[1] - 1, 1))
    brow = jnp.broadcast_to(b_ref[...].astype(jnp.float32), (filters, filters))
    r16 = lax.broadcasted_iota(jnp.int32, (filters, filters), 0)
    c16 = lax.broadcasted_iota(jnp.int32, (filters, filters), 1)
    bias = jnp.sum(jnp.where(r16 == c16, brow, 0.0), axis=1, keepdims=True)
    v = m + bias
    v = jnp.where(v > 0, v, slope * v).astype(jnp.bfloat16)
    r = lax.broadcasted_iota(jnp.int32, (m.shape[1], m.shape[1] // 2), 0)
    c = lax.broadcasted_iota(jnp.int32, (m.shape[1], m.shape[1] // 2), 1)
    pick = (r == 2 * c).astype(jnp.bfloat16)
    picked = jnp.dot(v, pick, preferred_element_type=jnp.float32).astype(o_ref.dtype)
    half = row // 2
    for zp in range(o_ref.shape[1]):
        for yp in range(o_ref.shape[2]):
            k = zp * o_ref.shape[2] + yp
            o_ref[:, zp, yp, :] = picked[:, k * half:(k + 1) * half]


def conv_pool(gathered, kernel, filter_bias, depth, height, across):
    filters = kernel.shape[0]
    weights = kernel.transpose(1, 2, 3, 0, 4)
    bias = filter_bias.reshape(1, filters)
    plane = height * across
    return pl.pallas_call(
        functools.partial(conv_kernel, plane=plane, row=across, depth=depth,
                          slabs=lax.axis_size("space")),
        out_shape=jax.ShapeDtypeStruct((filters, depth // 2, height // 2, across // 2), jnp.bfloat16),
        in_specs=[pl.BlockSpec(memory_space=pltpu.VMEM)] * 3,
        out_specs=pl.BlockSpec(memory_space=pltpu.VMEM),
        scratch_shapes=[
            pltpu.VMEM((2, filters, plane), jnp.float32),
            pltpu.VMEM((2, filters, plane), jnp.float32),
            pltpu.SemaphoreType.DMA((2,)),
            pltpu.SemaphoreType.DMA((2,)),
        ],
        compiler_params=pltpu.CompilerParams(collective_id=1, has_side_effects=True),
    )(gathered, weights, bias)


def on_device(volume, kernel, filter_bias):
    local_in, depth, height, across = volume.shape
    gathered = gather_filt(volume)
    return conv_pool(gathered, kernel, filter_bias, depth, height, across)


def solution(mesh):
    in_specs = (P("filt", "space", None, None), P("filt", None, None, None, None), P("filt"))
    out_specs = P("filt", "space", None, None)
    return jax.shard_map(
        on_device, mesh=mesh, in_specs=in_specs, out_specs=out_specs, check_vma=False
    )
```

```python
import functools

import jax
import jax.numpy as jnp
from jax import lax
from jax.experimental import pallas as pl
from jax.experimental.pallas import tpu as pltpu
from jax.sharding import PartitionSpec as P

slope = 0.3
MESH = pl.DeviceIdType.MESH


def gather_kernel(n, v_ref, out_ref, x_ref, local_sem, send_sem, fwd_sem, relay_sem, recv_sem):
    depth, height, across = v_ref.shape[1:]
    for z in range(depth):
        for y in range(height):
            x_ref[:, pl.ds((z * height + y) * across, across)] = v_ref[:, z, y, :]
    me = lax.axis_index("filt")
    sp = lax.axis_index("space")
    chips = n // 2
    zn = 4
    yn = chips // zn
    core = lax.rem(me, 2)
    chip = me // 2
    yy, zz = chip // zn, lax.rem(chip, zn)
    sib = me + 1 - 2 * core

    def dev(dy, dz):
        return (lax.rem(yy + dy + yn, yn) * zn + lax.rem(zz + dz + zn, zn)) * 2 + core

    direct = [(dy, dz) for dz in (1, 3, 0) for dy in range(yn) if (dy, dz) != (0, 0)]
    far = [(dy, 2) for dy in range(yn)]
    peers = [dev(dy, dz) for dy, dz in direct]
    rows, cols = x_ref.shape
    plane = cols // depth
    half = cols // 2

    def rows_of(slot):
        return pl.ds(pl.multiple_of(slot * rows, rows), rows)

    def main_at(slot):
        return out_ref.at[rows_of(slot)]

    barrier = pltpu.get_barrier_semaphore()
    for peer in [sib] + peers:
        pl.semaphore_signal(barrier, inc=1, device_id=(peer, sp), device_id_type=MESH)
    pl.semaphore_wait(barrier, 1 + len(peers))

    def copy(src, dst, sem, recv, dev_id):
        return pltpu.make_async_remote_copy(
            src_ref=src, dst_ref=dst, send_sem=sem, recv_sem=recv,
            device_id=dev_id, device_id_type=MESH,
        )

    def main_copy(src, slot, sem, dev_id):
        return copy(src, main_at(slot), sem, recv_sem.at[slot], (dev_id, sp))

    local = pltpu.make_async_copy(x_ref, main_at(me), local_sem.at[0])
    local.start()
    sends = [main_copy(x_ref, me, send_sem.at[0], sib)]
    for k, peer in enumerate(peers):
        sends.append(main_copy(x_ref, me, send_sem.at[k + 1], peer))
    for c in sends:
        c.start()
    forwards = []
    relays = []
    sources = []
    for k, (dy, dz) in enumerate(direct + far):
        src = dev(-dy, -dz)
        sources.append(src)
        main_copy(main_at(src), src, fwd_sem.at[0, k], src).wait_recv()
        if dz in (1, 3):
            part = pl.ds(0 if dz == 1 else half, half)
            held = out_ref.at[rows_of(src), part]
            target = dev(0, 1 if dz == 1 else -1)
            r = copy(held, held, relay_sem.at[dz // 2, dy], recv_sem.at[src], (target, sp))
            r.start()
            relays.append(r)
        c = main_copy(main_at(src), src, fwd_sem.at[0, k], sib)
        c.start()
        forwards.append(c)
    for k in range(chips):
        src = (sources[k - 1] if k else me) + 1 - 2 * core
        main_copy(main_at(src), src, fwd_sem.at[0, 0], sib).wait_recv()
    for c in sends + forwards + relays:
        c.wait_send()
    local.wait()


def gather_filt(block):
    n = lax.axis_size("filt")
    rows = block.shape[0]
    cols = block.size // rows
    chips = n // 2
    return pl.pallas_call(
        functools.partial(gather_kernel, n),
        out_shape=jax.ShapeDtypeStruct((n * rows, cols), block.dtype),
        in_specs=[pl.BlockSpec(memory_space=pltpu.VMEM)],
        out_specs=pl.BlockSpec(memory_space=pl.ANY),
        scratch_shapes=[
            pltpu.VMEM((rows, cols), block.dtype),
            pltpu.SemaphoreType.DMA((1,)),
            pltpu.SemaphoreType.DMA((chips,)),
            pltpu.SemaphoreType.DMA((1, chips)),
            pltpu.SemaphoreType.DMA((2, chips // 4)),
            pltpu.SemaphoreType.DMA((n,)),
        ],
        compiler_params=pltpu.CompilerParams(collective_id=0, has_side_effects=True),
    )(block)


def conv_kernel(g_ref, w_ref, b_ref, o_ref, send_buf, recv_buf, send_sem, recv_sem, *,
                plane, row, depth, slabs):
    sp = lax.axis_index("space")
    me = lax.axis_index("filt")
    has_lo = sp > 0
    has_hi = sp < slabs - 1
    barrier = pltpu.get_barrier_semaphore()

    @pl.when(has_lo)
    def _():
        pl.semaphore_signal(barrier, inc=1, device_id=(me, sp - 1), device_id_type=MESH)

    @pl.when(has_hi)
    def _():
        pl.semaphore_signal(barrier, inc=1, device_id=(me, sp + 1), device_id_type=MESH)

    g = g_ref[...]
    cols = g.shape[1]
    heights = plane // row
    x = lax.broadcasted_iota(jnp.int32, g.shape, 1) % row
    zero = jnp.zeros_like(g)
    left = jnp.where(x == 0, zero, pltpu.roll(g, 1, 1))
    right = jnp.where(x == row - 1, zero, pltpu.roll(g, cols - 1, 1))
    stacked = jnp.concatenate([left, g, right], axis=0)
    weights = jnp.concatenate(
        [jnp.concatenate([w_ref[a, b, c] for c in range(3)], axis=1)
         for a in range(3) for b in range(3)],
        axis=0,
    )
    filters = w_ref.shape[3]
    taps = 3 * filters
    edge_q = {
        (0, depth - 1): jnp.dot(weights[:taps], stacked[:, (depth - 1) * plane:],
                                preferred_element_type=jnp.float32),
        (2, 0): jnp.dot(weights[2 * taps:], stacked[:, :plane],
                        preferred_element_type=jnp.float32),
    }
    q = None

    def tap_row(a, b, p, y):
        if not 0 <= y < heights:
            return None
        if q is None:
            t = b * filters
            return edge_q[(a, p)][t:t + filters, y * row:(y + 1) * row]
        t = (a * 3 + b) * filters
        c0 = p * plane + y * row
        return q[t:t + filters, c0:c0 + row]

    def plane_sum(a, p):
        out = []
        for y in range(heights):
            parts = [tap_row(a, b, p, y + b - 1) for b in range(3)]
            parts = [v for v in parts if v is not None]
            total = parts[0]
            for v in parts[1:]:
                total = total + v
            out.append(total)
        return out

    send_buf[0] = jnp.concatenate(plane_sum(0, depth - 1), axis=1)
    send_buf[1] = jnp.concatenate(plane_sum(2, 0), axis=1)
    pl.semaphore_wait(barrier, has_lo.astype(jnp.int32) + has_hi.astype(jnp.int32))
    up = pltpu.make_async_remote_copy(
        src_ref=send_buf.at[0], dst_ref=recv_buf.at[0], send_sem=send_sem.at[0],
        recv_sem=recv_sem.at[0], device_id=(me, sp + 1), device_id_type=MESH,
    )
    down = pltpu.make_async_remote_copy(
        src_ref=send_buf.at[1], dst_ref=recv_buf.at[1], send_sem=send_sem.at[1],
        recv_sem=recv_sem.at[1], device_id=(me, sp - 1), device_id_type=MESH,
    )

    @pl.when(has_hi)
    def _():
        up.start()

    @pl.when(has_lo)
    def _():
        down.start()

    q = jnp.dot(weights, stacked, preferred_element_type=jnp.float32)
    acc = []
    for z in range(depth):
        rows_z = None
        for a in range(3):
            p = z + a - 1
            if not 0 <= p < depth:
                continue
            part = plane_sum(a, p)
            rows_z = part if rows_z is None else [u + v for u, v in zip(rows_z, part)]
        acc.append(rows_z)

    @pl.when(has_hi)
    def _():
        up.wait_send()
        down_recv = pltpu.make_async_remote_copy(
            src_ref=send_buf.at[1], dst_ref=recv_buf.at[1], send_sem=send_sem.at[1],
            recv_sem=recv_sem.at[1], device_id=(me, sp + 1), device_id_type=MESH,
        )
        down_recv.wait_recv()

    @pl.when(has_lo)
    def _():
        down.wait_send()
        up_recv = pltpu.make_async_remote_copy(
            src_ref=send_buf.at[0], dst_ref=recv_buf.at[0], send_sem=send_sem.at[0],
            recv_sem=recv_sem.at[0], device_id=(me, sp - 1), device_id_type=MESH,
        )
        up_recv.wait_recv()

    below = jnp.where(has_lo, recv_buf[0], 0.0)
    above = jnp.where(has_hi, recv_buf[1], 0.0)
    acc[0] = [v + below[:, y * row:(y + 1) * row] for y, v in enumerate(acc[0])]
    acc[depth - 1] = [v + above[:, y * row:(y + 1) * row] for y, v in enumerate(acc[depth - 1])]
    pooled = []
    for zp in range(depth // 2):
        zmax = [jnp.maximum(u, v) for u, v in zip(acc[2 * zp], acc[2 * zp + 1])]
        for yp in range(heights // 2):
            pooled.append(jnp.maximum(zmax[2 * yp], zmax[2 * yp + 1]))
    m = jnp.concatenate(pooled, axis=1)
    m = jnp.maximum(m, pltpu.roll(m, m.shape[1] - 1, 1))
    brow = jnp.broadcast_to(b_ref[...].astype(jnp.float32), (filters, filters))
    r16 = lax.broadcasted_iota(jnp.int32, (filters, filters), 0)
    c16 = lax.broadcasted_iota(jnp.int32, (filters, filters), 1)
    bias = jnp.sum(jnp.where(r16 == c16, brow, 0.0), axis=1, keepdims=True)
    v = m + bias
    v = jnp.where(v > 0, v, slope * v).astype(jnp.bfloat16)
    r = lax.broadcasted_iota(jnp.int32, (m.shape[1], m.shape[1] // 2), 0)
    c = lax.broadcasted_iota(jnp.int32, (m.shape[1], m.shape[1] // 2), 1)
    pick = (r == 2 * c).astype(jnp.bfloat16)
    picked = jnp.dot(v, pick, preferred_element_type=jnp.float32).astype(o_ref.dtype)
    half = row // 2
    for zp in range(o_ref.shape[1]):
        for yp in range(o_ref.shape[2]):
            k = zp * o_ref.shape[2] + yp
            o_ref[:, zp, yp, :] = picked[:, k * half:(k + 1) * half]


def conv_pool(gathered, kernel, filter_bias, depth, height, across):
    filters = kernel.shape[0]
    weights = kernel.transpose(1, 2, 3, 0, 4)
    bias = filter_bias.reshape(1, filters)
    plane = height * across
    return pl.pallas_call(
        functools.partial(conv_kernel, plane=plane, row=across, depth=depth,
                          slabs=lax.axis_size("space")),
        out_shape=jax.ShapeDtypeStruct((filters, depth // 2, height // 2, across // 2), jnp.bfloat16),
        in_specs=[pl.BlockSpec(memory_space=pltpu.VMEM)] * 3,
        out_specs=pl.BlockSpec(memory_space=pltpu.VMEM),
        scratch_shapes=[
            pltpu.VMEM((2, filters, plane), jnp.float32),
            pltpu.VMEM((2, filters, plane), jnp.float32),
            pltpu.SemaphoreType.DMA((2,)),
            pltpu.SemaphoreType.DMA((2,)),
        ],
        compiler_params=pltpu.CompilerParams(collective_id=1, has_side_effects=True),
    )(gathered, weights, bias)


def on_device(volume, kernel, filter_bias):
    local_in, depth, height, across = volume.shape
    gathered = gather_filt(volume)
    return conv_pool(gathered, kernel, filter_bias, depth, height, across)


def solution(mesh):
    in_specs = (P("filt", "space", None, None), P("filt", None, None, None, None), P("filt"))
    out_specs = P("filt", "space", None, None)
    return jax.shard_map(
        on_device, mesh=mesh, in_specs=in_specs, out_specs=out_specs, check_vma=False
    )
```

```python
import functools

import jax
import jax.numpy as jnp
from jax import lax
from jax.experimental import pallas as pl
from jax.experimental.pallas import tpu as pltpu
from jax.sharding import PartitionSpec as P

slope = 0.3
MESH = pl.DeviceIdType.MESH


def gather_kernel(n, slabs, v_ref, w_ref, out_ref, part_ref, x_ref, edge_in, send_buf,
                  recv_buf, local_sem, send_sem, fwd_sem, relay_sem, recv_sem, edge_sem,
                  part_send, part_recv):
    depth, height, across = v_ref.shape[1:]
    for z in range(depth):
        for y in range(height):
            x_ref[:, pl.ds((z * height + y) * across, across)] = v_ref[:, z, y, :]
    me = lax.axis_index("filt")
    sp = lax.axis_index("space")
    chips = n // 2
    zn = 4
    yn = chips // zn
    core = lax.rem(me, 2)
    chip = me // 2
    yy, zz = chip // zn, lax.rem(chip, zn)
    sib = me + 1 - 2 * core

    def dev(dy, dz):
        return (lax.rem(yy + dy + yn, yn) * zn + lax.rem(zz + dz + zn, zn)) * 2 + core

    direct = [(dy, dz) for dz in (1, 3, 0) for dy in range(yn) if (dy, dz) != (0, 0)]
    far = [(dy, 2) for dy in range(yn)]
    peers = [dev(dy, dz) for dy, dz in direct]
    rows, cols = x_ref.shape
    plane = cols // depth
    half = cols // 2

    def rows_of(slot):
        return pl.ds(pl.multiple_of(slot * rows, rows), rows)

    def main_at(slot):
        return out_ref.at[rows_of(slot)]

    barrier = pltpu.get_barrier_semaphore()
    for peer in [sib] + peers:
        pl.semaphore_signal(barrier, inc=1, device_id=(peer, sp), device_id_type=MESH)
    has_lo = sp > 0
    has_hi = sp < slabs - 1

    @pl.when(has_lo)
    def _():
        pl.semaphore_signal(barrier, inc=1, device_id=(me, sp - 1), device_id_type=MESH)

    @pl.when(has_hi)
    def _():
        pl.semaphore_signal(barrier, inc=1, device_id=(me, sp + 1), device_id_type=MESH)

    pl.semaphore_wait(
        barrier, 1 + len(peers) + has_lo.astype(jnp.int32) + has_hi.astype(jnp.int32)
    )

    def copy(src, dst, sem, recv, dev_id):
        return pltpu.make_async_remote_copy(
            src_ref=src, dst_ref=dst, send_sem=sem, recv_sem=recv,
            device_id=dev_id, device_id_type=MESH,
        )

    def main_copy(src, slot, sem, dev_id):
        return copy(src, main_at(slot), sem, recv_sem.at[slot], (dev_id, sp))

    local = pltpu.make_async_copy(x_ref, main_at(me), local_sem.at[0])
    local.start()
    sends = [main_copy(x_ref, me, send_sem.at[0], sib)]
    for k, peer in enumerate(peers):
        sends.append(main_copy(x_ref, me, send_sem.at[k + 1], peer))
    for c in sends:
        c.start()
    forwards = []
    relays = []
    sources = []
    for k, (dy, dz) in enumerate(direct + far):
        src = dev(-dy, -dz)
        sources.append(src)
        main_copy(main_at(src), src, fwd_sem.at[0, k], src).wait_recv()
        if dz in (1, 3):
            part = pl.ds(0 if dz == 1 else half, half)
            held = out_ref.at[rows_of(src), part]
            target = dev(0, 1 if dz == 1 else -1)
            r = copy(held, held, relay_sem.at[dz // 2, dy], recv_sem.at[src], (target, sp))
            r.start()
            relays.append(r)
        c = main_copy(main_at(src), src, fwd_sem.at[0, k], sib)
        c.start()
        forwards.append(c)
    for k in range(chips):
        src = (sources[k - 1] if k else me) + 1 - 2 * core
        main_copy(main_at(src), src, fwd_sem.at[0, 0], sib).wait_recv()
    local.wait()
    edges = []
    for k, p in enumerate((depth - 1, 0)):
        e = pltpu.make_async_copy(out_ref.at[:, pl.ds(p * plane, plane)], edge_in.at[k],
                                  edge_sem.at[k])
        e.start()
        edges.append(e)
    filters = w_ref.shape[3]
    for k, a in enumerate((0, 2)):
        edges[k].wait()
        g = edge_in[k]
        x = lax.broadcasted_iota(jnp.int32, g.shape, 1) % across
        zero = jnp.zeros_like(g)
        left = jnp.where(x == 0, zero, pltpu.roll(g, 1, 1))
        right = jnp.where(x == across - 1, zero, pltpu.roll(g, plane - 1, 1))
        stacked = jnp.concatenate([left, g, right], axis=0)
        weights = jnp.concatenate(
            [jnp.concatenate([w_ref[a, b, c] for c in range(3)], axis=1) for b in range(3)],
            axis=0,
        )
        q = jnp.dot(weights, stacked, preferred_element_type=jnp.float32)
        tiles = []
        for y in range(height):
            total = None
            for b in range(3):
                yi = y + b - 1
                if 0 <= yi < height:
                    v = q[b * filters:(b + 1) * filters, yi * across:(yi + 1) * across]
                    total = v if total is None else total + v
            tiles.append(total)
        send_buf[k] = jnp.concatenate(tiles, axis=1)
    up = pltpu.make_async_remote_copy(
        src_ref=send_buf.at[0], dst_ref=recv_buf.at[0], send_sem=part_send.at[0],
        recv_sem=part_recv.at[0], device_id=(me, sp + 1), device_id_type=MESH,
    )
    down = pltpu.make_async_remote_copy(
        src_ref=send_buf.at[1], dst_ref=recv_buf.at[1], send_sem=part_send.at[1],
        recv_sem=part_recv.at[1], device_id=(me, sp - 1), device_id_type=MESH,
    )

    @pl.when(has_hi)
    def _():
        up.start()

    @pl.when(has_lo)
    def _():
        down.start()

    for c in sends + forwards + relays:
        c.wait_send()

    @pl.when(has_hi)
    def _():
        up.wait_send()
        pltpu.make_async_remote_copy(
            src_ref=send_buf.at[1], dst_ref=recv_buf.at[1], send_sem=part_send.at[1],
            recv_sem=part_recv.at[1], device_id=(me, sp + 1), device_id_type=MESH,
        ).wait_recv()

    @pl.when(has_lo)
    def _():
        down.wait_send()
        pltpu.make_async_remote_copy(
            src_ref=send_buf.at[0], dst_ref=recv_buf.at[0], send_sem=part_send.at[0],
            recv_sem=part_recv.at[0], device_id=(me, sp - 1), device_id_type=MESH,
        ).wait_recv()

    part_ref[0] = jnp.where(has_lo, recv_buf[0], 0.0)
    part_ref[1] = jnp.where(has_hi, recv_buf[1], 0.0)


def gather_filt(block, weights):
    n = lax.axis_size("filt")
    slabs = lax.axis_size("space")
    rows = block.shape[0]
    cols = block.size // rows
    plane = cols // block.shape[1]
    filters = weights.shape[3]
    chips = n // 2
    return pl.pallas_call(
        functools.partial(gather_kernel, n, slabs),
        out_shape=(
            jax.ShapeDtypeStruct((n * rows, cols), block.dtype),
            jax.ShapeDtypeStruct((2, filters, plane), jnp.float32),
        ),
        in_specs=[pl.BlockSpec(memory_space=pltpu.VMEM)] * 2,
        out_specs=(pl.BlockSpec(memory_space=pl.ANY), pl.BlockSpec(memory_space=pltpu.VMEM)),
        scratch_shapes=[
            pltpu.VMEM((rows, cols), block.dtype),
            pltpu.VMEM((2, n * rows, plane), block.dtype),
            pltpu.VMEM((2, filters, plane), jnp.float32),
            pltpu.VMEM((2, filters, plane), jnp.float32),
            pltpu.SemaphoreType.DMA((1,)),
            pltpu.SemaphoreType.DMA((chips,)),
            pltpu.SemaphoreType.DMA((1, chips)),
            pltpu.SemaphoreType.DMA((2, chips // 4)),
            pltpu.SemaphoreType.DMA((n,)),
            pltpu.SemaphoreType.DMA((2,)),
            pltpu.SemaphoreType.DMA((2,)),
            pltpu.SemaphoreType.DMA((2,)),
        ],
        compiler_params=pltpu.CompilerParams(collective_id=0, has_side_effects=True),
    )(block, weights)


def conv_kernel(g_ref, w_ref, b_ref, p_ref, o_ref, *, plane, row, depth):
    g = g_ref[...]
    cols = g.shape[1]
    heights = plane // row
    x = lax.broadcasted_iota(jnp.int32, g.shape, 1) % row
    zero = jnp.zeros_like(g)
    left = jnp.where(x == 0, zero, pltpu.roll(g, 1, 1))
    right = jnp.where(x == row - 1, zero, pltpu.roll(g, cols - 1, 1))
    stacked = jnp.concatenate([left, g, right], axis=0)
    weights = jnp.concatenate(
        [jnp.concatenate([w_ref[a, b, c] for c in range(3)], axis=1)
         for a in range(3) for b in range(3)],
        axis=0,
    )
    filters = w_ref.shape[3]
    q = jnp.dot(weights, stacked, preferred_element_type=jnp.float32)

    def tap_row(a, b, p, y):
        if not 0 <= y < heights:
            return None
        t = (a * 3 + b) * filters
        c0 = p * plane + y * row
        return q[t:t + filters, c0:c0 + row]

    def plane_sum(a, p):
        out = []
        for y in range(heights):
            parts = [tap_row(a, b, p, y + b - 1) for b in range(3)]
            parts = [v for v in parts if v is not None]
            total = parts[0]
            for v in parts[1:]:
                total = total + v
            out.append(total)
        return out

    acc = []
    for z in range(depth):
        rows_z = None
        for a in range(3):
            p = z + a - 1
            if not 0 <= p < depth:
                continue
            part = plane_sum(a, p)
            rows_z = part if rows_z is None else [u + v for u, v in zip(rows_z, part)]
        acc.append(rows_z)

    below = p_ref[0]
    above = p_ref[1]
    acc[0] = [v + below[:, y * row:(y + 1) * row] for y, v in enumerate(acc[0])]
    acc[depth - 1] = [v + above[:, y * row:(y + 1) * row] for y, v in enumerate(acc[depth - 1])]
    pooled = []
    for zp in range(depth // 2):
        zmax = [jnp.maximum(u, v) for u, v in zip(acc[2 * zp], acc[2 * zp + 1])]
        for yp in range(heights // 2):
            pooled.append(jnp.maximum(zmax[2 * yp], zmax[2 * yp + 1]))
    m = jnp.concatenate(pooled, axis=1)
    m = jnp.maximum(m, pltpu.roll(m, m.shape[1] - 1, 1))
    brow = jnp.broadcast_to(b_ref[...].astype(jnp.float32), (filters, filters))
    r16 = lax.broadcasted_iota(jnp.int32, (filters, filters), 0)
    c16 = lax.broadcasted_iota(jnp.int32, (filters, filters), 1)
    bias = jnp.sum(jnp.where(r16 == c16, brow, 0.0), axis=1, keepdims=True)
    v = m + bias
    v = jnp.where(v > 0, v, slope * v).astype(jnp.bfloat16)
    r = lax.broadcasted_iota(jnp.int32, (m.shape[1], m.shape[1] // 2), 0)
    c = lax.broadcasted_iota(jnp.int32, (m.shape[1], m.shape[1] // 2), 1)
    pick = (r == 2 * c).astype(jnp.bfloat16)
    picked = jnp.dot(v, pick, preferred_element_type=jnp.float32).astype(o_ref.dtype)
    half = row // 2
    for zp in range(o_ref.shape[1]):
        for yp in range(o_ref.shape[2]):
            k = zp * o_ref.shape[2] + yp
            o_ref[:, zp, yp, :] = picked[:, k * half:(k + 1) * half]


def conv_pool(gathered, parts, weights, filter_bias, depth, height, across):
    filters = weights.shape[3]
    bias = filter_bias.reshape(1, filters)
    plane = height * across
    return pl.pallas_call(
        functools.partial(conv_kernel, plane=plane, row=across, depth=depth),
        out_shape=jax.ShapeDtypeStruct((filters, depth // 2, height // 2, across // 2), jnp.bfloat16),
        in_specs=[pl.BlockSpec(memory_space=pltpu.VMEM)] * 4,
        out_specs=pl.BlockSpec(memory_space=pltpu.VMEM),
    )(gathered, weights, bias, parts)


def on_device(volume, kernel, filter_bias):
    local_in, depth, height, across = volume.shape
    weights = kernel.transpose(1, 2, 3, 0, 4)
    gathered, parts = gather_filt(volume, weights)
    return conv_pool(gathered, parts, weights, filter_bias, depth, height, across)


def solution(mesh):
    in_specs = (P("filt", "space", None, None), P("filt", None, None, None, None), P("filt"))
    out_specs = P("filt", "space", None, None)
    return jax.shard_map(
        on_device, mesh=mesh, in_specs=in_specs, out_specs=out_specs, check_vma=False
    )
```

```python
import functools

import jax
import jax.numpy as jnp
from jax import lax
from jax.experimental import pallas as pl
from jax.experimental.pallas import tpu as pltpu
from jax.sharding import PartitionSpec as P

slope = 0.3
MESH = pl.DeviceIdType.MESH


def gather_kernel(n, slabs, v_ref, w_ref, acc_ref, part_ref, out_ref, x_ref, send_buf,
                  recv_buf, local_sem, send_sem, fwd_sem, relay_sem, recv_sem,
                  part_send, part_recv):
    depth, height, across = v_ref.shape[1:]
    for z in range(depth):
        for y in range(height):
            x_ref[:, pl.ds((z * height + y) * across, across)] = v_ref[:, z, y, :]
    me = lax.axis_index("filt")
    sp = lax.axis_index("space")
    chips = n // 2
    zn = 4
    yn = chips // zn
    core = lax.rem(me, 2)
    chip = me // 2
    yy, zz = chip // zn, lax.rem(chip, zn)
    sib = me + 1 - 2 * core

    def dev(dy, dz):
        return (lax.rem(yy + dy + yn, yn) * zn + lax.rem(zz + dz + zn, zn)) * 2 + core

    direct = [(dy, dz) for dz in (1, 3, 0) for dy in range(yn) if (dy, dz) != (0, 0)]
    far = [(dy, 2) for dy in range(yn)]
    peers = [dev(dy, dz) for dy, dz in direct]
    rows, cols = x_ref.shape
    plane = cols // depth
    half = cols // 2

    def rows_of(slot):
        return pl.ds(pl.multiple_of(slot * rows, rows), rows)

    def main_at(slot):
        return out_ref.at[rows_of(slot)]

    barrier = pltpu.get_barrier_semaphore()
    for peer in [sib] + peers:
        pl.semaphore_signal(barrier, inc=1, device_id=(peer, sp), device_id_type=MESH)
    has_lo = sp > 0
    has_hi = sp < slabs - 1

    @pl.when(has_lo)
    def _():
        pl.semaphore_signal(barrier, inc=1, device_id=(me, sp - 1), device_id_type=MESH)

    @pl.when(has_hi)
    def _():
        pl.semaphore_signal(barrier, inc=1, device_id=(me, sp + 1), device_id_type=MESH)

    pl.semaphore_wait(
        barrier, 1 + len(peers) + has_lo.astype(jnp.int32) + has_hi.astype(jnp.int32)
    )

    def copy(src, dst, sem, recv, dev_id):
        return pltpu.make_async_remote_copy(
            src_ref=src, dst_ref=dst, send_sem=sem, recv_sem=recv,
            device_id=dev_id, device_id_type=MESH,
        )

    def main_copy(src, slot, sem, dev_id):
        return copy(src, main_at(slot), sem, recv_sem.at[slot], (dev_id, sp))

    local = pltpu.make_async_copy(x_ref, main_at(me), local_sem.at[0])
    local.start()
    sends = [main_copy(x_ref, me, send_sem.at[0], sib)]
    for k, peer in enumerate(peers):
        sends.append(main_copy(x_ref, me, send_sem.at[k + 1], peer))
    for c in sends:
        c.start()
    forwards = []
    relays = []
    sources = []
    for k, (dy, dz) in enumerate(direct + far):
        src = dev(-dy, -dz)
        sources.append(src)
        main_copy(main_at(src), src, fwd_sem.at[0, k], src).wait_recv()
        if dz in (1, 3):
            part = pl.ds(0 if dz == 1 else half, half)
            held = out_ref.at[rows_of(src), part]
            target = dev(0, 1 if dz == 1 else -1)
            r = copy(held, held, relay_sem.at[dz // 2, dy], recv_sem.at[src], (target, sp))
            r.start()
            relays.append(r)
        c = main_copy(main_at(src), src, fwd_sem.at[0, k], sib)
        c.start()
        forwards.append(c)
    for k in range(chips):
        src = (sources[k - 1] if k else me) + 1 - 2 * core
        main_copy(main_at(src), src, fwd_sem.at[0, 0], sib).wait_recv()
    local.wait()
    filters = w_ref.shape[3]
    for k, (a, p) in enumerate(((0, depth - 1), (2, 0))):
        g = out_ref[:, pl.ds(p * plane, plane)]
        x = lax.broadcasted_iota(jnp.int32, g.shape, 1) % across
        zero = jnp.zeros_like(g)
        left = jnp.where(x == 0, zero, pltpu.roll(g, 1, 1))
        right = jnp.where(x == across - 1, zero, pltpu.roll(g, plane - 1, 1))
        stacked = jnp.concatenate([left, g, right], axis=0)
        weights = jnp.concatenate(
            [jnp.concatenate([w_ref[a, b, c] for c in range(3)], axis=1) for b in range(3)],
            axis=0,
        )
        q = jnp.dot(weights, stacked, preferred_element_type=jnp.float32)
        tiles = []
        for y in range(height):
            total = None
            for b in range(3):
                yi = y + b - 1
                if 0 <= yi < height:
                    v = q[b * filters:(b + 1) * filters, yi * across:(yi + 1) * across]
                    total = v if total is None else total + v
            tiles.append(total)
        send_buf[k] = jnp.concatenate(tiles, axis=1)
    up = pltpu.make_async_remote_copy(
        src_ref=send_buf.at[0], dst_ref=recv_buf.at[0], send_sem=part_send.at[0],
        recv_sem=part_recv.at[0], device_id=(me, sp + 1), device_id_type=MESH,
    )
    down = pltpu.make_async_remote_copy(
        src_ref=send_buf.at[1], dst_ref=recv_buf.at[1], send_sem=part_send.at[1],
        recv_sem=part_recv.at[1], device_id=(me, sp - 1), device_id_type=MESH,
    )

    @pl.when(has_hi)
    def _():
        up.start()

    @pl.when(has_lo)
    def _():
        down.start()

    acc_ref[...] = interior_conv(out_ref, w_ref, plane=plane, row=across, depth=depth)
    for c in sends + forwards + relays:
        c.wait_send()

    @pl.when(has_hi)
    def _():
        up.wait_send()
        pltpu.make_async_remote_copy(
            src_ref=send_buf.at[1], dst_ref=recv_buf.at[1], send_sem=part_send.at[1],
            recv_sem=part_recv.at[1], device_id=(me, sp + 1), device_id_type=MESH,
        ).wait_recv()

    @pl.when(has_lo)
    def _():
        down.wait_send()
        pltpu.make_async_remote_copy(
            src_ref=send_buf.at[0], dst_ref=recv_buf.at[0], send_sem=part_send.at[0],
            recv_sem=part_recv.at[0], device_id=(me, sp - 1), device_id_type=MESH,
        ).wait_recv()

    part_ref[0] = jnp.where(has_lo, recv_buf[0], 0.0)
    part_ref[1] = jnp.where(has_hi, recv_buf[1], 0.0)


def gather_filt(block, weights):
    n = lax.axis_size("filt")
    slabs = lax.axis_size("space")
    rows = block.shape[0]
    cols = block.size // rows
    plane = cols // block.shape[1]
    filters = weights.shape[3]
    chips = n // 2
    return pl.pallas_call(
        functools.partial(gather_kernel, n, slabs),
        out_shape=(
            jax.ShapeDtypeStruct((filters, cols), jnp.float32),
            jax.ShapeDtypeStruct((2, filters, plane), jnp.float32),
        ),
        in_specs=[pl.BlockSpec(memory_space=pltpu.VMEM)] * 2,
        out_specs=(pl.BlockSpec(memory_space=pltpu.VMEM), pl.BlockSpec(memory_space=pltpu.VMEM)),
        scratch_shapes=[
            pltpu.VMEM((n * rows, cols), block.dtype),
            pltpu.VMEM((rows, cols), block.dtype),
            pltpu.VMEM((2, filters, plane), jnp.float32),
            pltpu.VMEM((2, filters, plane), jnp.float32),
            pltpu.SemaphoreType.DMA((1,)),
            pltpu.SemaphoreType.DMA((chips,)),
            pltpu.SemaphoreType.DMA((1, chips)),
            pltpu.SemaphoreType.DMA((2, chips // 4)),
            pltpu.SemaphoreType.DMA((n,)),
            pltpu.SemaphoreType.DMA((2,)),
            pltpu.SemaphoreType.DMA((2,)),
        ],
        compiler_params=pltpu.CompilerParams(collective_id=0, has_side_effects=True),
    )(block, weights)


def interior_conv(g_ref, w_ref, *, plane, row, depth):
    g = g_ref[...]
    cols = g.shape[1]
    heights = plane // row
    x = lax.broadcasted_iota(jnp.int32, g.shape, 1) % row
    zero = jnp.zeros_like(g)
    left = jnp.where(x == 0, zero, pltpu.roll(g, 1, 1))
    right = jnp.where(x == row - 1, zero, pltpu.roll(g, cols - 1, 1))
    stacked = jnp.concatenate([left, g, right], axis=0)
    weights = jnp.concatenate(
        [jnp.concatenate([w_ref[a, b, c] for c in range(3)], axis=1)
         for a in range(3) for b in range(3)],
        axis=0,
    )
    filters = w_ref.shape[3]
    q = jnp.dot(weights, stacked, preferred_element_type=jnp.float32)

    def tap_row(a, b, p, y):
        if not 0 <= y < heights:
            return None
        t = (a * 3 + b) * filters
        c0 = p * plane + y * row
        return q[t:t + filters, c0:c0 + row]

    tiles = []
    for z in range(depth):
        for y in range(heights):
            total = None
            for a in range(3):
                p = z + a - 1
                if not 0 <= p < depth:
                    continue
                for b in range(3):
                    v = tap_row(a, b, p, y + b - 1)
                    if v is not None:
                        total = v if total is None else total + v
            tiles.append(total)
    return jnp.concatenate(tiles, axis=1)


def finish_kernel(acc_ref, p_ref, b_ref, o_ref, *, plane, row, depth):
    filters = acc_ref.shape[0]
    heights = plane // row
    acc = [[acc_ref[:, pl.ds((z * heights + y) * row, row)] for y in range(heights)]
           for z in range(depth)]
    below = p_ref[0]
    above = p_ref[1]
    acc[0] = [v + below[:, y * row:(y + 1) * row] for y, v in enumerate(acc[0])]
    acc[depth - 1] = [v + above[:, y * row:(y + 1) * row] for y, v in enumerate(acc[depth - 1])]
    pooled = []
    for zp in range(depth // 2):
        zmax = [jnp.maximum(u, v) for u, v in zip(acc[2 * zp], acc[2 * zp + 1])]
        for yp in range(heights // 2):
            pooled.append(jnp.maximum(zmax[2 * yp], zmax[2 * yp + 1]))
    m = jnp.concatenate(pooled, axis=1)
    m = jnp.maximum(m, pltpu.roll(m, m.shape[1] - 1, 1))
    brow = jnp.broadcast_to(b_ref[...].astype(jnp.float32), (filters, filters))
    r16 = lax.broadcasted_iota(jnp.int32, (filters, filters), 0)
    c16 = lax.broadcasted_iota(jnp.int32, (filters, filters), 1)
    bias = jnp.sum(jnp.where(r16 == c16, brow, 0.0), axis=1, keepdims=True)
    v = m + bias
    v = jnp.where(v > 0, v, slope * v).astype(jnp.bfloat16)
    r = lax.broadcasted_iota(jnp.int32, (m.shape[1], m.shape[1] // 2), 0)
    c = lax.broadcasted_iota(jnp.int32, (m.shape[1], m.shape[1] // 2), 1)
    pick = (r == 2 * c).astype(jnp.bfloat16)
    picked = jnp.dot(v, pick, preferred_element_type=jnp.float32).astype(o_ref.dtype)
    half = row // 2
    for zp in range(o_ref.shape[1]):
        for yp in range(o_ref.shape[2]):
            k = zp * o_ref.shape[2] + yp
            o_ref[:, zp, yp, :] = picked[:, k * half:(k + 1) * half]


def on_device(volume, kernel, filter_bias):
    local_in, depth, height, across = volume.shape
    weights = kernel.transpose(1, 2, 3, 0, 4)
    acc, parts = gather_filt(volume, weights)
    filters = weights.shape[3]
    return pl.pallas_call(
        functools.partial(finish_kernel, plane=height * across, row=across, depth=depth),
        out_shape=jax.ShapeDtypeStruct((filters, depth // 2, height // 2, across // 2), jnp.bfloat16),
        in_specs=[pl.BlockSpec(memory_space=pltpu.VMEM)] * 3,
        out_specs=pl.BlockSpec(memory_space=pltpu.VMEM),
    )(acc, parts, filter_bias.reshape(1, filters))


def solution(mesh):
    in_specs = (P("filt", "space", None, None), P("filt", None, None, None, None), P("filt"))
    out_specs = P("filt", "space", None, None)
    return jax.shard_map(
        on_device, mesh=mesh, in_specs=in_specs, out_specs=out_specs, check_vma=False
    )
```

```python
import functools

import jax
import jax.numpy as jnp
from jax import lax
from jax.experimental import pallas as pl
from jax.experimental.pallas import tpu as pltpu
from jax.sharding import PartitionSpec as P

slope = 0.3
MESH = pl.DeviceIdType.MESH


def gather_kernel(n, slabs, v_ref, w_ref, acc_ref, part_ref, out_ref, x_ref, send_buf,
                  recv_buf, local_sem, send_sem, fwd_sem, relay_sem, recv_sem,
                  part_send, part_recv, half_recv, send2_sem):
    depth, height, across = v_ref.shape[1:]
    for z in range(depth):
        for y in range(height):
            x_ref[:, pl.ds((z * height + y) * across, across)] = v_ref[:, z, y, :]
    me = lax.axis_index("filt")
    sp = lax.axis_index("space")
    chips = n // 2
    zn = 4
    yn = chips // zn
    core = lax.rem(me, 2)
    chip = me // 2
    yy, zz = chip // zn, lax.rem(chip, zn)
    sib = me + 1 - 2 * core

    def dev(dy, dz):
        return (lax.rem(yy + dy + yn, yn) * zn + lax.rem(zz + dz + zn, zn)) * 2 + core

    direct = [(dy, dz) for dz in (1, 3, 0) for dy in range(yn) if (dy, dz) != (0, 0)]
    far = [(dy, 2) for dy in range(yn)]
    peers = [dev(dy, dz) for dy, dz in direct]
    rows, cols = x_ref.shape
    plane = cols // depth
    half = cols // 2

    def rows_of(slot):
        return pl.ds(pl.multiple_of(slot * rows, rows), rows)

    def main_at(slot):
        return out_ref.at[rows_of(slot)]

    barrier = pltpu.get_barrier_semaphore()
    for peer in [sib] + peers:
        pl.semaphore_signal(barrier, inc=1, device_id=(peer, sp), device_id_type=MESH)
    has_lo = sp > 0
    has_hi = sp < slabs - 1

    @pl.when(has_lo)
    def _():
        pl.semaphore_signal(barrier, inc=1, device_id=(me, sp - 1), device_id_type=MESH)

    @pl.when(has_hi)
    def _():
        pl.semaphore_signal(barrier, inc=1, device_id=(me, sp + 1), device_id_type=MESH)

    pl.semaphore_wait(
        barrier, 1 + len(peers) + has_lo.astype(jnp.int32) + has_hi.astype(jnp.int32)
    )

    def copy(src, dst, sem, recv, dev_id):
        return pltpu.make_async_remote_copy(
            src_ref=src, dst_ref=dst, send_sem=sem, recv_sem=recv,
            device_id=dev_id, device_id_type=MESH,
        )

    def main_copy(src, slot, sem, dev_id):
        return copy(src, main_at(slot), sem, recv_sem.at[slot], (dev_id, sp))

    local = pltpu.make_async_copy(x_ref, main_at(me), local_sem.at[0])
    local.start()
    sends = [main_copy(x_ref, me, send_sem.at[0], sib)]
    later = []
    for k, ((dy, dz), peer) in enumerate(zip(direct, peers)):
        if dz in (1, 3):
            first = pl.ds(0 if dz == 1 else half, half)
            rest = pl.ds(half if dz == 1 else 0, half)
            dst = out_ref.at[rows_of(me), first]
            sends.append(copy(x_ref.at[:, first], dst, send_sem.at[k + 1], half_recv.at[me],
                              (peer, sp)))
            dst = out_ref.at[rows_of(me), rest]
            later.append(copy(x_ref.at[:, rest], dst, send2_sem.at[k], recv_sem.at[me],
                              (peer, sp)))
        else:
            later.append(main_copy(x_ref, me, send_sem.at[k + 1], peer))
    sends += later
    for c in sends:
        c.start()
    forwards = []
    relays = []
    sources = []
    for dy, dz in direct:
        if dz in (1, 3):
            src = dev(-dy, -dz)
            part = pl.ds(0 if dz == 1 else half, half)
            held = out_ref.at[rows_of(src), part]
            copy(held, held, relay_sem.at[dz // 2, dy], half_recv.at[src], (src, sp)).wait_recv()
            target = dev(0, 1 if dz == 1 else -1)
            r = copy(held, held, relay_sem.at[dz // 2, dy], recv_sem.at[src], (target, sp))
            r.start()
            relays.append(r)
    for k, (dy, dz) in enumerate(direct + far):
        src = dev(-dy, -dz)
        sources.append(src)
        if dz in (1, 3):
            rest = pl.ds(half if dz == 1 else 0, half)
            held = out_ref.at[rows_of(src), rest]
            copy(held, held, fwd_sem.at[0, k], recv_sem.at[src], (src, sp)).wait_recv()
        else:
            main_copy(main_at(src), src, fwd_sem.at[0, k], src).wait_recv()
        c = main_copy(main_at(src), src, fwd_sem.at[0, k], sib)
        c.start()
        forwards.append(c)
    for k in range(chips):
        src = (sources[k - 1] if k else me) + 1 - 2 * core
        main_copy(main_at(src), src, fwd_sem.at[0, 0], sib).wait_recv()
    local.wait()
    filters = w_ref.shape[3]
    for k, (a, p) in enumerate(((0, depth - 1), (2, 0))):
        g = out_ref[:, pl.ds(p * plane, plane)]
        x = lax.broadcasted_iota(jnp.int32, g.shape, 1) % across
        zero = jnp.zeros_like(g)
        left = jnp.where(x == 0, zero, pltpu.roll(g, 1, 1))
        right = jnp.where(x == across - 1, zero, pltpu.roll(g, plane - 1, 1))
        stacked = jnp.concatenate([left, g, right], axis=0)
        weights = jnp.concatenate(
            [jnp.concatenate([w_ref[a, b, c] for c in range(3)], axis=1) for b in range(3)],
            axis=0,
        )
        q = jnp.dot(weights, stacked, preferred_element_type=jnp.float32)
        tiles = []
        for y in range(height):
            total = None
            for b in range(3):
                yi = y + b - 1
                if 0 <= yi < height:
                    v = q[b * filters:(b + 1) * filters, yi * across:(yi + 1) * across]
                    total = v if total is None else total + v
            tiles.append(total)
        send_buf[k] = jnp.concatenate(tiles, axis=1)
    up = pltpu.make_async_remote_copy(
        src_ref=send_buf.at[0], dst_ref=recv_buf.at[0], send_sem=part_send.at[0],
        recv_sem=part_recv.at[0], device_id=(me, sp + 1), device_id_type=MESH,
    )
    down = pltpu.make_async_remote_copy(
        src_ref=send_buf.at[1], dst_ref=recv_buf.at[1], send_sem=part_send.at[1],
        recv_sem=part_recv.at[1], device_id=(me, sp - 1), device_id_type=MESH,
    )

    @pl.when(has_hi)
    def _():
        up.start()

    @pl.when(has_lo)
    def _():
        down.start()

    acc_ref[...] = interior_conv(out_ref, w_ref, plane=plane, row=across, depth=depth)
    for c in sends + forwards + relays:
        c.wait_send()

    @pl.when(has_hi)
    def _():
        up.wait_send()
        pltpu.make_async_remote_copy(
            src_ref=send_buf.at[1], dst_ref=recv_buf.at[1], send_sem=part_send.at[1],
            recv_sem=part_recv.at[1], device_id=(me, sp + 1), device_id_type=MESH,
        ).wait_recv()

    @pl.when(has_lo)
    def _():
        down.wait_send()
        pltpu.make_async_remote_copy(
            src_ref=send_buf.at[0], dst_ref=recv_buf.at[0], send_sem=part_send.at[0],
            recv_sem=part_recv.at[0], device_id=(me, sp - 1), device_id_type=MESH,
        ).wait_recv()

    part_ref[0] = jnp.where(has_lo, recv_buf[0], 0.0)
    part_ref[1] = jnp.where(has_hi, recv_buf[1], 0.0)


def gather_filt(block, weights):
    n = lax.axis_size("filt")
    slabs = lax.axis_size("space")
    rows = block.shape[0]
    cols = block.size // rows
    plane = cols // block.shape[1]
    filters = weights.shape[3]
    chips = n // 2
    return pl.pallas_call(
        functools.partial(gather_kernel, n, slabs),
        out_shape=(
            jax.ShapeDtypeStruct((filters, cols), jnp.float32),
            jax.ShapeDtypeStruct((2, filters, plane), jnp.float32),
        ),
        in_specs=[pl.BlockSpec(memory_space=pltpu.VMEM)] * 2,
        out_specs=(pl.BlockSpec(memory_space=pltpu.VMEM), pl.BlockSpec(memory_space=pltpu.VMEM)),
        scratch_shapes=[
            pltpu.VMEM((n * rows, cols), block.dtype),
            pltpu.VMEM((rows, cols), block.dtype),
            pltpu.VMEM((2, filters, plane), jnp.float32),
            pltpu.VMEM((2, filters, plane), jnp.float32),
            pltpu.SemaphoreType.DMA((1,)),
            pltpu.SemaphoreType.DMA((chips,)),
            pltpu.SemaphoreType.DMA((1, chips)),
            pltpu.SemaphoreType.DMA((2, chips // 4)),
            pltpu.SemaphoreType.DMA((n,)),
            pltpu.SemaphoreType.DMA((2,)),
            pltpu.SemaphoreType.DMA((2,)),
            pltpu.SemaphoreType.DMA((n,)),
            pltpu.SemaphoreType.DMA((chips,)),
        ],
        compiler_params=pltpu.CompilerParams(collective_id=0, has_side_effects=True),
    )(block, weights)


def interior_conv(g_ref, w_ref, *, plane, row, depth):
    g = g_ref[...]
    cols = g.shape[1]
    heights = plane // row
    x = lax.broadcasted_iota(jnp.int32, g.shape, 1) % row
    zero = jnp.zeros_like(g)
    left = jnp.where(x == 0, zero, pltpu.roll(g, 1, 1))
    right = jnp.where(x == row - 1, zero, pltpu.roll(g, cols - 1, 1))
    stacked = jnp.concatenate([left, g, right], axis=0)
    weights = jnp.concatenate(
        [jnp.concatenate([w_ref[a, b, c] for c in range(3)], axis=1)
         for a in range(3) for b in range(3)],
        axis=0,
    )
    filters = w_ref.shape[3]
    q = jnp.dot(weights, stacked, preferred_element_type=jnp.float32)

    def tap_row(a, b, p, y):
        if not 0 <= y < heights:
            return None
        t = (a * 3 + b) * filters
        c0 = p * plane + y * row
        return q[t:t + filters, c0:c0 + row]

    tiles = []
    for z in range(depth):
        for y in range(heights):
            total = None
            for a in range(3):
                p = z + a - 1
                if not 0 <= p < depth:
                    continue
                for b in range(3):
                    v = tap_row(a, b, p, y + b - 1)
                    if v is not None:
                        total = v if total is None else total + v
            tiles.append(total)
    return jnp.concatenate(tiles, axis=1)


def finish_kernel(acc_ref, p_ref, b_ref, o_ref, *, plane, row, depth):
    filters = acc_ref.shape[0]
    heights = plane // row
    acc = [[acc_ref[:, pl.ds((z * heights + y) * row, row)] for y in range(heights)]
           for z in range(depth)]
    below = p_ref[0]
    above = p_ref[1]
    acc[0] = [v + below[:, y * row:(y + 1) * row] for y, v in enumerate(acc[0])]
    acc[depth - 1] = [v + above[:, y * row:(y + 1) * row] for y, v in enumerate(acc[depth - 1])]
    pooled = []
    for zp in range(depth // 2):
        zmax = [jnp.maximum(u, v) for u, v in zip(acc[2 * zp], acc[2 * zp + 1])]
        for yp in range(heights // 2):
            pooled.append(jnp.maximum(zmax[2 * yp], zmax[2 * yp + 1]))
    m = jnp.concatenate(pooled, axis=1)
    m = jnp.maximum(m, pltpu.roll(m, m.shape[1] - 1, 1))
    brow = jnp.broadcast_to(b_ref[...].astype(jnp.float32), (filters, filters))
    r16 = lax.broadcasted_iota(jnp.int32, (filters, filters), 0)
    c16 = lax.broadcasted_iota(jnp.int32, (filters, filters), 1)
    bias = jnp.sum(jnp.where(r16 == c16, brow, 0.0), axis=1, keepdims=True)
    v = m + bias
    v = jnp.where(v > 0, v, slope * v).astype(jnp.bfloat16)
    r = lax.broadcasted_iota(jnp.int32, (m.shape[1], m.shape[1] // 2), 0)
    c = lax.broadcasted_iota(jnp.int32, (m.shape[1], m.shape[1] // 2), 1)
    pick = (r == 2 * c).astype(jnp.bfloat16)
    picked = jnp.dot(v, pick, preferred_element_type=jnp.float32).astype(o_ref.dtype)
    half = row // 2
    for zp in range(o_ref.shape[1]):
        for yp in range(o_ref.shape[2]):
            k = zp * o_ref.shape[2] + yp
            o_ref[:, zp, yp, :] = picked[:, k * half:(k + 1) * half]


def on_device(volume, kernel, filter_bias):
    local_in, depth, height, across = volume.shape
    weights = kernel.transpose(1, 2, 3, 0, 4)
    acc, parts = gather_filt(volume, weights)
    filters = weights.shape[3]
    return pl.pallas_call(
        functools.partial(finish_kernel, plane=height * across, row=across, depth=depth),
        out_shape=jax.ShapeDtypeStruct((filters, depth // 2, height // 2, across // 2), jnp.bfloat16),
        in_specs=[pl.BlockSpec(memory_space=pltpu.VMEM)] * 3,
        out_specs=pl.BlockSpec(memory_space=pltpu.VMEM),
    )(acc, parts, filter_bias.reshape(1, filters))


def solution(mesh):
    in_specs = (P("filt", "space", None, None), P("filt", None, None, None, None), P("filt"))
    out_specs = P("filt", "space", None, None)
    return jax.shard_map(
        on_device, mesh=mesh, in_specs=in_specs, out_specs=out_specs, check_vma=False
    )
```

```python
import functools

import jax
import jax.numpy as jnp
from jax import lax
from jax.experimental import pallas as pl
from jax.experimental.pallas import tpu as pltpu
from jax.sharding import PartitionSpec as P

slope = 0.3
MESH = pl.DeviceIdType.MESH


def gather_kernel(n, slabs, v_ref, w_ref, b_ref, o_ref, acc_ref, part_ref, out_ref, x_ref, send_buf,
                  recv_buf, local_sem, send_sem, fwd_sem, relay_sem, recv_sem,
                  part_send, part_recv, half_recv, send2_sem):
    depth, height, across = v_ref.shape[1:]
    for z in range(depth):
        for y in range(height):
            x_ref[:, pl.ds((z * height + y) * across, across)] = v_ref[:, z, y, :]
    me = lax.axis_index("filt")
    sp = lax.axis_index("space")
    chips = n // 2
    zn = 4
    yn = chips // zn
    core = lax.rem(me, 2)
    chip = me // 2
    yy, zz = chip // zn, lax.rem(chip, zn)
    sib = me + 1 - 2 * core

    def dev(dy, dz):
        return (lax.rem(yy + dy + yn, yn) * zn + lax.rem(zz + dz + zn, zn)) * 2 + core

    direct = [(dy, dz) for dz in (1, 3, 0) for dy in range(yn) if (dy, dz) != (0, 0)]
    far = [(dy, 2) for dy in range(yn)]
    peers = [dev(dy, dz) for dy, dz in direct]
    rows, cols = x_ref.shape
    plane = cols // depth
    half = cols // 2

    def rows_of(slot):
        return pl.ds(pl.multiple_of(slot * rows, rows), rows)

    def main_at(slot):
        return out_ref.at[rows_of(slot)]

    barrier = pltpu.get_barrier_semaphore()
    for peer in [sib] + peers:
        pl.semaphore_signal(barrier, inc=1, device_id=(peer, sp), device_id_type=MESH)
    has_lo = sp > 0
    has_hi = sp < slabs - 1

    @pl.when(has_lo)
    def _():
        pl.semaphore_signal(barrier, inc=1, device_id=(me, sp - 1), device_id_type=MESH)

    @pl.when(has_hi)
    def _():
        pl.semaphore_signal(barrier, inc=1, device_id=(me, sp + 1), device_id_type=MESH)

    pl.semaphore_wait(
        barrier, 1 + len(peers) + has_lo.astype(jnp.int32) + has_hi.astype(jnp.int32)
    )

    def copy(src, dst, sem, recv, dev_id):
        return pltpu.make_async_remote_copy(
            src_ref=src, dst_ref=dst, send_sem=sem, recv_sem=recv,
            device_id=dev_id, device_id_type=MESH,
        )

    def main_copy(src, slot, sem, dev_id):
        return copy(src, main_at(slot), sem, recv_sem.at[slot], (dev_id, sp))

    local = pltpu.make_async_copy(x_ref, main_at(me), local_sem.at[0])
    local.start()
    sends = [main_copy(x_ref, me, send_sem.at[0], sib)]
    later = []
    for k, ((dy, dz), peer) in enumerate(zip(direct, peers)):
        if dz in (1, 3):
            first = pl.ds(0 if dz == 1 else half, half)
            rest = pl.ds(half if dz == 1 else 0, half)
            dst = out_ref.at[rows_of(me), first]
            sends.append(copy(x_ref.at[:, first], dst, send_sem.at[k + 1], half_recv.at[me],
                              (peer, sp)))
            dst = out_ref.at[rows_of(me), rest]
            later.append(copy(x_ref.at[:, rest], dst, send2_sem.at[k], recv_sem.at[me],
                              (peer, sp)))
        else:
            later.append(main_copy(x_ref, me, send_sem.at[k + 1], peer))
    sends += later
    for c in sends:
        c.start()
    forwards = []
    relays = []
    sources = []
    for dy, dz in direct:
        if dz in (1, 3):
            src = dev(-dy, -dz)
            part = pl.ds(0 if dz == 1 else half, half)
            held = out_ref.at[rows_of(src), part]
            copy(held, held, relay_sem.at[dz // 2, dy], half_recv.at[src], (src, sp)).wait_recv()
            target = dev(0, 1 if dz == 1 else -1)
            r = copy(held, held, relay_sem.at[dz // 2, dy], recv_sem.at[src], (target, sp))
            r.start()
            relays.append(r)
    for k, (dy, dz) in enumerate(direct + far):
        src = dev(-dy, -dz)
        sources.append(src)
        if dz in (1, 3):
            rest = pl.ds(half if dz == 1 else 0, half)
            held = out_ref.at[rows_of(src), rest]
            copy(held, held, fwd_sem.at[0, k], recv_sem.at[src], (src, sp)).wait_recv()
        else:
            main_copy(main_at(src), src, fwd_sem.at[0, k], src).wait_recv()
        c = main_copy(main_at(src), src, fwd_sem.at[0, k], sib)
        c.start()
        forwards.append(c)
    for k in range(chips):
        src = (sources[k - 1] if k else me) + 1 - 2 * core
        main_copy(main_at(src), src, fwd_sem.at[0, 0], sib).wait_recv()
    local.wait()
    filters = w_ref.shape[3]
    for k, (a, p) in enumerate(((0, depth - 1), (2, 0))):
        g = out_ref[:, pl.ds(p * plane, plane)]
        x = lax.broadcasted_iota(jnp.int32, g.shape, 1) % across
        zero = jnp.zeros_like(g)
        left = jnp.where(x == 0, zero, pltpu.roll(g, 1, 1))
        right = jnp.where(x == across - 1, zero, pltpu.roll(g, plane - 1, 1))
        stacked = jnp.concatenate([left, g, right], axis=0)
        weights = jnp.concatenate(
            [jnp.concatenate([w_ref[a, b, c] for c in range(3)], axis=1) for b in range(3)],
            axis=0,
        )
        q = jnp.dot(weights, stacked, preferred_element_type=jnp.float32)
        tiles = []
        for y in range(height):
            total = None
            for b in range(3):
                yi = y + b - 1
                if 0 <= yi < height:
                    v = q[b * filters:(b + 1) * filters, yi * across:(yi + 1) * across]
                    total = v if total is None else total + v
            tiles.append(total)
        send_buf[k] = jnp.concatenate(tiles, axis=1)
    up = pltpu.make_async_remote_copy(
        src_ref=send_buf.at[0], dst_ref=recv_buf.at[0], send_sem=part_send.at[0],
        recv_sem=part_recv.at[0], device_id=(me, sp + 1), device_id_type=MESH,
    )
    down = pltpu.make_async_remote_copy(
        src_ref=send_buf.at[1], dst_ref=recv_buf.at[1], send_sem=part_send.at[1],
        recv_sem=part_recv.at[1], device_id=(me, sp - 1), device_id_type=MESH,
    )

    @pl.when(has_hi)
    def _():
        up.start()

    @pl.when(has_lo)
    def _():
        down.start()

    acc_ref[...] = interior_conv(out_ref, w_ref, plane=plane, row=across, depth=depth)
    for c in sends + forwards + relays:
        c.wait_send()

    @pl.when(has_hi)
    def _():
        up.wait_send()
        pltpu.make_async_remote_copy(
            src_ref=send_buf.at[1], dst_ref=recv_buf.at[1], send_sem=part_send.at[1],
            recv_sem=part_recv.at[1], device_id=(me, sp + 1), device_id_type=MESH,
        ).wait_recv()

    @pl.when(has_lo)
    def _():
        down.wait_send()
        pltpu.make_async_remote_copy(
            src_ref=send_buf.at[0], dst_ref=recv_buf.at[0], send_sem=part_send.at[0],
            recv_sem=part_recv.at[0], device_id=(me, sp - 1), device_id_type=MESH,
        ).wait_recv()

    part_ref[0] = jnp.where(has_lo, recv_buf[0], 0.0)
    part_ref[1] = jnp.where(has_hi, recv_buf[1], 0.0)
    finish_kernel(acc_ref, part_ref, b_ref, o_ref, plane=plane, row=across, depth=depth)


def gather_filt(block, weights, bias):
    n = lax.axis_size("filt")
    slabs = lax.axis_size("space")
    rows, depth, height, across = block.shape
    cols = block.size // rows
    plane = cols // depth
    filters = weights.shape[3]
    chips = n // 2
    return pl.pallas_call(
        functools.partial(gather_kernel, n, slabs),
        out_shape=jax.ShapeDtypeStruct((filters, depth // 2, height // 2, across // 2), jnp.bfloat16),
        in_specs=[pl.BlockSpec(memory_space=pltpu.VMEM)] * 3,
        out_specs=pl.BlockSpec(memory_space=pltpu.VMEM),
        scratch_shapes=[
            pltpu.VMEM((filters, cols), jnp.float32),
            pltpu.VMEM((2, filters, plane), jnp.float32),
            pltpu.VMEM((n * rows, cols), block.dtype),
            pltpu.VMEM((rows, cols), block.dtype),
            pltpu.VMEM((2, filters, plane), jnp.float32),
            pltpu.VMEM((2, filters, plane), jnp.float32),
            pltpu.SemaphoreType.DMA((1,)),
            pltpu.SemaphoreType.DMA((chips,)),
            pltpu.SemaphoreType.DMA((1, chips)),
            pltpu.SemaphoreType.DMA((2, chips // 4)),
            pltpu.SemaphoreType.DMA((n,)),
            pltpu.SemaphoreType.DMA((2,)),
            pltpu.SemaphoreType.DMA((2,)),
            pltpu.SemaphoreType.DMA((n,)),
            pltpu.SemaphoreType.DMA((chips,)),
        ],
        compiler_params=pltpu.CompilerParams(collective_id=0, has_side_effects=True),
    )(block, weights, bias)


def interior_conv(g_ref, w_ref, *, plane, row, depth):
    g = g_ref[...]
    cols = g.shape[1]
    heights = plane // row
    x = lax.broadcasted_iota(jnp.int32, g.shape, 1) % row
    zero = jnp.zeros_like(g)
    left = jnp.where(x == 0, zero, pltpu.roll(g, 1, 1))
    right = jnp.where(x == row - 1, zero, pltpu.roll(g, cols - 1, 1))
    stacked = jnp.concatenate([left, g, right], axis=0)
    weights = jnp.concatenate(
        [jnp.concatenate([w_ref[a, b, c] for c in range(3)], axis=1)
         for a in range(3) for b in range(3)],
        axis=0,
    )
    filters = w_ref.shape[3]
    q = jnp.dot(weights, stacked, preferred_element_type=jnp.float32)

    def tap_row(a, b, p, y):
        if not 0 <= y < heights:
            return None
        t = (a * 3 + b) * filters
        c0 = p * plane + y * row
        return q[t:t + filters, c0:c0 + row]

    tiles = []
    for z in range(depth):
        for y in range(heights):
            total = None
            for a in range(3):
                p = z + a - 1
                if not 0 <= p < depth:
                    continue
                for b in range(3):
                    v = tap_row(a, b, p, y + b - 1)
                    if v is not None:
                        total = v if total is None else total + v
            tiles.append(total)
    return jnp.concatenate(tiles, axis=1)


def finish_kernel(acc_ref, p_ref, b_ref, o_ref, *, plane, row, depth):
    filters = acc_ref.shape[0]
    heights = plane // row
    acc = [[acc_ref[:, pl.ds((z * heights + y) * row, row)] for y in range(heights)]
           for z in range(depth)]
    below = p_ref[0]
    above = p_ref[1]
    acc[0] = [v + below[:, y * row:(y + 1) * row] for y, v in enumerate(acc[0])]
    acc[depth - 1] = [v + above[:, y * row:(y + 1) * row] for y, v in enumerate(acc[depth - 1])]
    pooled = []
    for zp in range(depth // 2):
        zmax = [jnp.maximum(u, v) for u, v in zip(acc[2 * zp], acc[2 * zp + 1])]
        for yp in range(heights // 2):
            pooled.append(jnp.maximum(zmax[2 * yp], zmax[2 * yp + 1]))
    m = jnp.concatenate(pooled, axis=1)
    m = jnp.maximum(m, pltpu.roll(m, m.shape[1] - 1, 1))
    brow = jnp.broadcast_to(b_ref[...].astype(jnp.float32), (filters, filters))
    r16 = lax.broadcasted_iota(jnp.int32, (filters, filters), 0)
    c16 = lax.broadcasted_iota(jnp.int32, (filters, filters), 1)
    bias = jnp.sum(jnp.where(r16 == c16, brow, 0.0), axis=1, keepdims=True)
    v = m + bias
    v = jnp.where(v > 0, v, slope * v).astype(jnp.bfloat16)
    r = lax.broadcasted_iota(jnp.int32, (m.shape[1], m.shape[1] // 2), 0)
    c = lax.broadcasted_iota(jnp.int32, (m.shape[1], m.shape[1] // 2), 1)
    pick = (r == 2 * c).astype(jnp.bfloat16)
    picked = jnp.dot(v, pick, preferred_element_type=jnp.float32).astype(o_ref.dtype)
    half = row // 2
    for zp in range(o_ref.shape[1]):
        for yp in range(o_ref.shape[2]):
            k = zp * o_ref.shape[2] + yp
            o_ref[:, zp, yp, :] = picked[:, k * half:(k + 1) * half]


def on_device(volume, kernel, filter_bias):
    local_in, depth, height, across = volume.shape
    weights = kernel.transpose(1, 2, 3, 0, 4)
    return gather_filt(volume, weights, filter_bias.reshape(1, -1))


def solution(mesh):
    in_specs = (P("filt", "space", None, None), P("filt", None, None, None, None), P("filt"))
    out_specs = P("filt", "space", None, None)
    return jax.shard_map(
        on_device, mesh=mesh, in_specs=in_specs, out_specs=out_specs, check_vma=False
    )
```

```python
import functools

import jax
import jax.numpy as jnp
from jax import lax
from jax.experimental import pallas as pl
from jax.experimental.pallas import tpu as pltpu
from jax.sharding import PartitionSpec as P

slope = 0.3
MESH = pl.DeviceIdType.MESH


def gather_kernel(n, slabs, v_ref, w_ref, b_ref, o_ref, acc_ref, part_ref, out_ref, x_ref, send_buf,
                  recv_buf, local_sem, send_sem, fwd_sem, relay_sem, recv_sem,
                  part_send, part_recv, half_recv, send2_sem):
    depth, height, across = v_ref.shape[1:]
    for z in range(depth):
        for y in range(height):
            x_ref[:, pl.ds((z * height + y) * across, across)] = v_ref[:, z, y, :]
    me = lax.axis_index("filt")
    sp = lax.axis_index("space")
    chips = n // 2
    zn = 4
    yn = chips // zn
    core = lax.rem(me, 2)
    chip = me // 2
    yy, zz = chip // zn, lax.rem(chip, zn)
    sib = me + 1 - 2 * core

    def dev(dy, dz):
        return (lax.rem(yy + dy + yn, yn) * zn + lax.rem(zz + dz + zn, zn)) * 2 + core

    direct = [(dy, dz) for dz in (1, 3, 0) for dy in range(yn) if (dy, dz) != (0, 0)]
    far = [(dy, 2) for dy in range(yn)]
    peers = [dev(dy, dz) for dy, dz in direct]
    rows, cols = x_ref.shape
    plane = cols // depth
    half = cols // 2

    def rows_of(slot):
        return pl.ds(pl.multiple_of(slot * rows, rows), rows)

    def main_at(slot):
        return out_ref.at[rows_of(slot)]

    barrier = pltpu.get_barrier_semaphore()
    for peer in [sib] + peers:
        pl.semaphore_signal(barrier, inc=1, device_id=(peer, sp), device_id_type=MESH)
    has_lo = sp > 0
    has_hi = sp < slabs - 1

    @pl.when(has_lo)
    def _():
        pl.semaphore_signal(barrier, inc=1, device_id=(me, sp - 1), device_id_type=MESH)

    @pl.when(has_hi)
    def _():
        pl.semaphore_signal(barrier, inc=1, device_id=(me, sp + 1), device_id_type=MESH)

    pl.semaphore_wait(
        barrier, 1 + len(peers) + has_lo.astype(jnp.int32) + has_hi.astype(jnp.int32)
    )

    def copy(src, dst, sem, recv, dev_id):
        return pltpu.make_async_remote_copy(
            src_ref=src, dst_ref=dst, send_sem=sem, recv_sem=recv,
            device_id=dev_id, device_id_type=MESH,
        )

    def main_copy(src, slot, sem, dev_id):
        return copy(src, main_at(slot), sem, recv_sem.at[slot], (dev_id, sp))

    local = pltpu.make_async_copy(x_ref, main_at(me), local_sem.at[0])
    sends = [main_copy(x_ref, me, send_sem.at[0], sib)]
    later = []
    for k, ((dy, dz), peer) in enumerate(zip(direct, peers)):
        if dz in (1, 3):
            first = pl.ds(0 if dz == 1 else half, half)
            rest = pl.ds(half if dz == 1 else 0, half)
            dst = out_ref.at[rows_of(me), first]
            sends.append(copy(x_ref.at[:, first], dst, send_sem.at[k + 1], half_recv.at[me],
                              (peer, sp)))
            dst = out_ref.at[rows_of(me), rest]
            later.append(copy(x_ref.at[:, rest], dst, send2_sem.at[k], recv_sem.at[me],
                              (peer, sp)))
        else:
            later.append(main_copy(x_ref, me, send_sem.at[k + 1], peer))
    sends = sends[1:] + later + sends[:1]
    for c in sends:
        c.start()
    local.start()
    forwards = []
    relays = []
    sources = []
    for dy, dz in direct:
        if dz in (1, 3):
            src = dev(-dy, -dz)
            part = pl.ds(0 if dz == 1 else half, half)
            held = out_ref.at[rows_of(src), part]
            copy(held, held, relay_sem.at[dz // 2, dy], half_recv.at[src], (src, sp)).wait_recv()
            target = dev(0, 1 if dz == 1 else -1)
            r = copy(held, held, relay_sem.at[dz // 2, dy], recv_sem.at[src], (target, sp))
            r.start()
            relays.append(r)
    for k, (dy, dz) in enumerate(direct + far):
        src = dev(-dy, -dz)
        sources.append(src)
        if dz in (1, 3):
            rest = pl.ds(half if dz == 1 else 0, half)
            held = out_ref.at[rows_of(src), rest]
            copy(held, held, fwd_sem.at[0, k], recv_sem.at[src], (src, sp)).wait_recv()
        else:
            main_copy(main_at(src), src, fwd_sem.at[0, k], src).wait_recv()
        c = main_copy(main_at(src), src, fwd_sem.at[0, k], sib)
        c.start()
        forwards.append(c)
    for k in range(chips):
        src = (sources[k - 1] if k else me) + 1 - 2 * core
        main_copy(main_at(src), src, fwd_sem.at[0, 0], sib).wait_recv()
    local.wait()
    filters = w_ref.shape[3]
    for k, (a, p) in enumerate(((0, depth - 1), (2, 0))):
        g = out_ref[:, pl.ds(p * plane, plane)]
        x = lax.broadcasted_iota(jnp.int32, g.shape, 1) % across
        zero = jnp.zeros_like(g)
        left = jnp.where(x == 0, zero, pltpu.roll(g, 1, 1))
        right = jnp.where(x == across - 1, zero, pltpu.roll(g, plane - 1, 1))
        stacked = jnp.concatenate([left, g, right], axis=0)
        weights = jnp.concatenate(
            [jnp.concatenate([w_ref[a, b, c] for c in range(3)], axis=1) for b in range(3)],
            axis=0,
        )
        q = jnp.dot(weights, stacked, preferred_element_type=jnp.float32)
        tiles = []
        for y in range(height):
            total = None
            for b in range(3):
                yi = y + b - 1
                if 0 <= yi < height:
                    v = q[b * filters:(b + 1) * filters, yi * across:(yi + 1) * across]
                    total = v if total is None else total + v
            tiles.append(total)
        send_buf[k] = jnp.concatenate(tiles, axis=1)
    up = pltpu.make_async_remote_copy(
        src_ref=send_buf.at[0], dst_ref=recv_buf.at[0], send_sem=part_send.at[0],
        recv_sem=part_recv.at[0], device_id=(me, sp + 1), device_id_type=MESH,
    )
    down = pltpu.make_async_remote_copy(
        src_ref=send_buf.at[1], dst_ref=recv_buf.at[1], send_sem=part_send.at[1],
        recv_sem=part_recv.at[1], device_id=(me, sp - 1), device_id_type=MESH,
    )

    @pl.when(has_hi)
    def _():
        up.start()

    @pl.when(has_lo)
    def _():
        down.start()

    acc_ref[...] = interior_conv(out_ref, w_ref, plane=plane, row=across, depth=depth)
    for c in sends + forwards + relays:
        c.wait_send()

    @pl.when(has_hi)
    def _():
        up.wait_send()
        pltpu.make_async_remote_copy(
            src_ref=send_buf.at[1], dst_ref=recv_buf.at[1], send_sem=part_send.at[1],
            recv_sem=part_recv.at[1], device_id=(me, sp + 1), device_id_type=MESH,
        ).wait_recv()

    @pl.when(has_lo)
    def _():
        down.wait_send()
        pltpu.make_async_remote_copy(
            src_ref=send_buf.at[0], dst_ref=recv_buf.at[0], send_sem=part_send.at[0],
            recv_sem=part_recv.at[0], device_id=(me, sp - 1), device_id_type=MESH,
        ).wait_recv()

    part_ref[0] = jnp.where(has_lo, recv_buf[0], 0.0)
    part_ref[1] = jnp.where(has_hi, recv_buf[1], 0.0)
    finish_kernel(acc_ref, part_ref, b_ref, o_ref, plane=plane, row=across, depth=depth)


def gather_filt(block, weights, bias):
    n = lax.axis_size("filt")
    slabs = lax.axis_size("space")
    rows, depth, height, across = block.shape
    cols = block.size // rows
    plane = cols // depth
    filters = weights.shape[3]
    chips = n // 2
    return pl.pallas_call(
        functools.partial(gather_kernel, n, slabs),
        out_shape=jax.ShapeDtypeStruct((filters, depth // 2, height // 2, across // 2), jnp.bfloat16),
        in_specs=[pl.BlockSpec(memory_space=pltpu.VMEM)] * 3,
        out_specs=pl.BlockSpec(memory_space=pltpu.VMEM),
        scratch_shapes=[
            pltpu.VMEM((filters, cols), jnp.float32),
            pltpu.VMEM((2, filters, plane), jnp.float32),
            pltpu.VMEM((n * rows, cols), block.dtype),
            pltpu.VMEM((rows, cols), block.dtype),
            pltpu.VMEM((2, filters, plane), jnp.float32),
            pltpu.VMEM((2, filters, plane), jnp.float32),
            pltpu.SemaphoreType.DMA((1,)),
            pltpu.SemaphoreType.DMA((chips,)),
            pltpu.SemaphoreType.DMA((1, chips)),
            pltpu.SemaphoreType.DMA((2, chips // 4)),
            pltpu.SemaphoreType.DMA((n,)),
            pltpu.SemaphoreType.DMA((2,)),
            pltpu.SemaphoreType.DMA((2,)),
            pltpu.SemaphoreType.DMA((n,)),
            pltpu.SemaphoreType.DMA((chips,)),
        ],
        compiler_params=pltpu.CompilerParams(collective_id=0, has_side_effects=True),
    )(block, weights, bias)


def interior_conv(g_ref, w_ref, *, plane, row, depth):
    g = g_ref[...]
    cols = g.shape[1]
    heights = plane // row
    x = lax.broadcasted_iota(jnp.int32, g.shape, 1) % row
    zero = jnp.zeros_like(g)
    left = jnp.where(x == 0, zero, pltpu.roll(g, 1, 1))
    right = jnp.where(x == row - 1, zero, pltpu.roll(g, cols - 1, 1))
    stacked = jnp.concatenate([left, g, right], axis=0)
    weights = jnp.concatenate(
        [jnp.concatenate([w_ref[a, b, c] for c in range(3)], axis=1)
         for a in range(3) for b in range(3)],
        axis=0,
    )
    filters = w_ref.shape[3]
    q = jnp.dot(weights, stacked, preferred_element_type=jnp.float32)

    def tap_row(a, b, p, y):
        if not 0 <= y < heights:
            return None
        t = (a * 3 + b) * filters
        c0 = p * plane + y * row
        return q[t:t + filters, c0:c0 + row]

    tiles = []
    for z in range(depth):
        for y in range(heights):
            total = None
            for a in range(3):
                p = z + a - 1
                if not 0 <= p < depth:
                    continue
                for b in range(3):
                    v = tap_row(a, b, p, y + b - 1)
                    if v is not None:
                        total = v if total is None else total + v
            tiles.append(total)
    return jnp.concatenate(tiles, axis=1)


def finish_kernel(acc_ref, p_ref, b_ref, o_ref, *, plane, row, depth):
    filters = acc_ref.shape[0]
    heights = plane // row
    acc = [[acc_ref[:, pl.ds((z * heights + y) * row, row)] for y in range(heights)]
           for z in range(depth)]
    below = p_ref[0]
    above = p_ref[1]
    acc[0] = [v + below[:, y * row:(y + 1) * row] for y, v in enumerate(acc[0])]
    acc[depth - 1] = [v + above[:, y * row:(y + 1) * row] for y, v in enumerate(acc[depth - 1])]
    pooled = []
    for zp in range(depth // 2):
        zmax = [jnp.maximum(u, v) for u, v in zip(acc[2 * zp], acc[2 * zp + 1])]
        for yp in range(heights // 2):
            pooled.append(jnp.maximum(zmax[2 * yp], zmax[2 * yp + 1]))
    m = jnp.concatenate(pooled, axis=1)
    m = jnp.maximum(m, pltpu.roll(m, m.shape[1] - 1, 1))
    brow = jnp.broadcast_to(b_ref[...].astype(jnp.float32), (filters, filters))
    r16 = lax.broadcasted_iota(jnp.int32, (filters, filters), 0)
    c16 = lax.broadcasted_iota(jnp.int32, (filters, filters), 1)
    bias = jnp.sum(jnp.where(r16 == c16, brow, 0.0), axis=1, keepdims=True)
    v = m + bias
    v = jnp.where(v > 0, v, slope * v).astype(jnp.bfloat16)
    r = lax.broadcasted_iota(jnp.int32, (m.shape[1], m.shape[1] // 2), 0)
    c = lax.broadcasted_iota(jnp.int32, (m.shape[1], m.shape[1] // 2), 1)
    pick = (r == 2 * c).astype(jnp.bfloat16)
    picked = jnp.dot(v, pick, preferred_element_type=jnp.float32).astype(o_ref.dtype)
    half = row // 2
    for zp in range(o_ref.shape[1]):
        for yp in range(o_ref.shape[2]):
            k = zp * o_ref.shape[2] + yp
            o_ref[:, zp, yp, :] = picked[:, k * half:(k + 1) * half]


def on_device(volume, kernel, filter_bias):
    local_in, depth, height, across = volume.shape
    weights = kernel.transpose(1, 2, 3, 0, 4)
    return gather_filt(volume, weights, filter_bias.reshape(1, -1))


def solution(mesh):
    in_specs = (P("filt", "space", None, None), P("filt", None, None, None, None), P("filt"))
    out_specs = P("filt", "space", None, None)
    return jax.shard_map(
        on_device, mesh=mesh, in_specs=in_specs, out_specs=out_specs, check_vma=False
    )
```

```python
import functools

import jax
import jax.numpy as jnp
from jax import lax
from jax.experimental import pallas as pl
from jax.experimental.pallas import tpu as pltpu
from jax.sharding import PartitionSpec as P

slope = 0.3
MESH = pl.DeviceIdType.MESH


def gather_kernel(n, slabs, v_ref, w_hbm, b_ref, o_ref, acc_ref, part_ref, out_ref, x_ref, send_buf,
                  recv_buf, local_sem, send_sem, fwd_sem, relay_sem, recv_sem,
                  part_send, part_recv, half_recv, send2_sem, w_ref, w_sem, wmat):
    depth, height, across = v_ref.shape[1:]
    for z in range(depth):
        for y in range(height):
            x_ref[:, pl.ds((z * height + y) * across, across)] = v_ref[:, z, y, :]
    me = lax.axis_index("filt")
    sp = lax.axis_index("space")
    chips = n // 2
    zn = 4
    yn = chips // zn
    core = lax.rem(me, 2)
    chip = me // 2
    yy, zz = chip // zn, lax.rem(chip, zn)
    sib = me + 1 - 2 * core

    def dev(dy, dz):
        return (lax.rem(yy + dy + yn, yn) * zn + lax.rem(zz + dz + zn, zn)) * 2 + core

    direct = [(dy, dz) for dz in (1, 3, 0) for dy in range(yn) if (dy, dz) != (0, 0)]
    far = [(dy, 2) for dy in range(yn)]
    peers = [dev(dy, dz) for dy, dz in direct]
    rows, cols = x_ref.shape
    plane = cols // depth
    half = cols // 2

    def rows_of(slot):
        return pl.ds(pl.multiple_of(slot * rows, rows), rows)

    def main_at(slot):
        return out_ref.at[rows_of(slot)]

    barrier = pltpu.get_barrier_semaphore()
    for peer in [sib] + peers:
        pl.semaphore_signal(barrier, inc=1, device_id=(peer, sp), device_id_type=MESH)
    w_copy = pltpu.make_async_copy(w_hbm, w_ref, w_sem.at[0])
    w_copy.start()
    w_copy.wait()
    wmat[...] = jnp.concatenate(
        [jnp.concatenate([w_ref[a, b, c] for c in range(3)], axis=1)
         for a in range(3) for b in range(3)],
        axis=0,
    )
    has_lo = sp > 0
    has_hi = sp < slabs - 1

    @pl.when(has_lo)
    def _():
        pl.semaphore_signal(barrier, inc=1, device_id=(me, sp - 1), device_id_type=MESH)

    @pl.when(has_hi)
    def _():
        pl.semaphore_signal(barrier, inc=1, device_id=(me, sp + 1), device_id_type=MESH)

    pl.semaphore_wait(
        barrier, 1 + len(peers) + has_lo.astype(jnp.int32) + has_hi.astype(jnp.int32)
    )

    def copy(src, dst, sem, recv, dev_id):
        return pltpu.make_async_remote_copy(
            src_ref=src, dst_ref=dst, send_sem=sem, recv_sem=recv,
            device_id=dev_id, device_id_type=MESH,
        )

    def main_copy(src, slot, sem, dev_id):
        return copy(src, main_at(slot), sem, recv_sem.at[slot], (dev_id, sp))

    local = pltpu.make_async_copy(x_ref, main_at(me), local_sem.at[0])
    sends = [main_copy(x_ref, me, send_sem.at[0], sib)]
    later = []
    for k, ((dy, dz), peer) in enumerate(zip(direct, peers)):
        if dz in (1, 3):
            first = pl.ds(0 if dz == 1 else half, half)
            rest = pl.ds(half if dz == 1 else 0, half)
            dst = out_ref.at[rows_of(me), first]
            sends.append(copy(x_ref.at[:, first], dst, send_sem.at[k + 1], half_recv.at[me],
                              (peer, sp)))
            dst = out_ref.at[rows_of(me), rest]
            later.append(copy(x_ref.at[:, rest], dst, send2_sem.at[k], recv_sem.at[me],
                              (peer, sp)))
        else:
            later.append(main_copy(x_ref, me, send_sem.at[k + 1], peer))
    sends = sends[1:] + later + sends[:1]
    for c in sends:
        c.start()
    local.start()
    forwards = []
    relays = []
    sources = []
    for dy, dz in direct:
        if dz in (1, 3):
            src = dev(-dy, -dz)
            part = pl.ds(0 if dz == 1 else half, half)
            held = out_ref.at[rows_of(src), part]
            copy(held, held, relay_sem.at[dz // 2, dy], half_recv.at[src], (src, sp)).wait_recv()
            target = dev(0, 1 if dz == 1 else -1)
            r = copy(held, held, relay_sem.at[dz // 2, dy], recv_sem.at[src], (target, sp))
            r.start()
            relays.append(r)
    for k, (dy, dz) in enumerate(direct + far):
        src = dev(-dy, -dz)
        sources.append(src)
        if dz in (1, 3):
            rest = pl.ds(half if dz == 1 else 0, half)
            held = out_ref.at[rows_of(src), rest]
            copy(held, held, fwd_sem.at[0, k], recv_sem.at[src], (src, sp)).wait_recv()
        else:
            main_copy(main_at(src), src, fwd_sem.at[0, k], src).wait_recv()
        c = main_copy(main_at(src), src, fwd_sem.at[0, k], sib)
        c.start()
        forwards.append(c)
    for k in range(chips):
        src = (sources[k - 1] if k else me) + 1 - 2 * core
        main_copy(main_at(src), src, fwd_sem.at[0, 0], sib).wait_recv()
    local.wait()
    filters = w_ref.shape[3]
    for k, (a, p) in enumerate(((0, depth - 1), (2, 0))):
        g = out_ref[:, pl.ds(p * plane, plane)]
        x = lax.broadcasted_iota(jnp.int32, g.shape, 1) % across
        zero = jnp.zeros_like(g)
        left = jnp.where(x == 0, zero, pltpu.roll(g, 1, 1))
        right = jnp.where(x == across - 1, zero, pltpu.roll(g, plane - 1, 1))
        stacked = jnp.concatenate([left, g, right], axis=0)
        rows3 = 3 * w_ref.shape[3]
        q = jnp.dot(wmat[a * rows3:(a + 1) * rows3], stacked, preferred_element_type=jnp.float32)
        tiles = []
        for y in range(height):
            total = None
            for b in range(3):
                yi = y + b - 1
                if 0 <= yi < height:
                    v = q[b * filters:(b + 1) * filters, yi * across:(yi + 1) * across]
                    total = v if total is None else total + v
            tiles.append(total)
        send_buf[k] = jnp.concatenate(tiles, axis=1)
    up = pltpu.make_async_remote_copy(
        src_ref=send_buf.at[0], dst_ref=recv_buf.at[0], send_sem=part_send.at[0],
        recv_sem=part_recv.at[0], device_id=(me, sp + 1), device_id_type=MESH,
    )
    down = pltpu.make_async_remote_copy(
        src_ref=send_buf.at[1], dst_ref=recv_buf.at[1], send_sem=part_send.at[1],
        recv_sem=part_recv.at[1], device_id=(me, sp - 1), device_id_type=MESH,
    )

    @pl.when(has_hi)
    def _():
        up.start()

    @pl.when(has_lo)
    def _():
        down.start()

    acc_ref[...] = interior_conv(out_ref, wmat, w_ref.shape[3], plane=plane, row=across, depth=depth)
    for c in sends + forwards + relays:
        c.wait_send()

    @pl.when(has_hi)
    def _():
        up.wait_send()
        pltpu.make_async_remote_copy(
            src_ref=send_buf.at[1], dst_ref=recv_buf.at[1], send_sem=part_send.at[1],
            recv_sem=part_recv.at[1], device_id=(me, sp + 1), device_id_type=MESH,
        ).wait_recv()

    @pl.when(has_lo)
    def _():
        down.wait_send()
        pltpu.make_async_remote_copy(
            src_ref=send_buf.at[0], dst_ref=recv_buf.at[0], send_sem=part_send.at[0],
            recv_sem=part_recv.at[0], device_id=(me, sp - 1), device_id_type=MESH,
        ).wait_recv()

    part_ref[0] = jnp.where(has_lo, recv_buf[0], 0.0)
    part_ref[1] = jnp.where(has_hi, recv_buf[1], 0.0)
    finish_kernel(acc_ref, part_ref, b_ref, o_ref, plane=plane, row=across, depth=depth)


def gather_filt(block, weights, bias):
    n = lax.axis_size("filt")
    slabs = lax.axis_size("space")
    rows, depth, height, across = block.shape
    cols = block.size // rows
    plane = cols // depth
    filters = weights.shape[3]
    chips = n // 2
    return pl.pallas_call(
        functools.partial(gather_kernel, n, slabs),
        out_shape=jax.ShapeDtypeStruct((filters, depth // 2, height // 2, across // 2), jnp.bfloat16),
        in_specs=[
            pl.BlockSpec(memory_space=pltpu.VMEM),
            pl.BlockSpec(memory_space=pl.ANY),
            pl.BlockSpec(memory_space=pltpu.VMEM),
        ],
        out_specs=pl.BlockSpec(memory_space=pltpu.VMEM),
        scratch_shapes=[
            pltpu.VMEM((filters, cols), jnp.float32),
            pltpu.VMEM((2, filters, plane), jnp.float32),
            pltpu.VMEM((n * rows, cols), block.dtype),
            pltpu.VMEM((rows, cols), block.dtype),
            pltpu.VMEM((2, filters, plane), jnp.float32),
            pltpu.VMEM((2, filters, plane), jnp.float32),
            pltpu.SemaphoreType.DMA((1,)),
            pltpu.SemaphoreType.DMA((chips,)),
            pltpu.SemaphoreType.DMA((1, chips)),
            pltpu.SemaphoreType.DMA((2, chips // 4)),
            pltpu.SemaphoreType.DMA((n,)),
            pltpu.SemaphoreType.DMA((2,)),
            pltpu.SemaphoreType.DMA((2,)),
            pltpu.SemaphoreType.DMA((n,)),
            pltpu.SemaphoreType.DMA((chips,)),
            pltpu.VMEM(weights.shape, weights.dtype),
            pltpu.SemaphoreType.DMA((1,)),
            pltpu.VMEM((9 * filters, 3 * weights.shape[4]), weights.dtype),
        ],
        compiler_params=pltpu.CompilerParams(collective_id=0, has_side_effects=True),
    )(block, weights, bias)


def interior_conv(g_ref, wmat, filters, *, plane, row, depth):
    g = g_ref[...]
    cols = g.shape[1]
    heights = plane // row
    x = lax.broadcasted_iota(jnp.int32, g.shape, 1) % row
    zero = jnp.zeros_like(g)
    left = jnp.where(x == 0, zero, pltpu.roll(g, 1, 1))
    right = jnp.where(x == row - 1, zero, pltpu.roll(g, cols - 1, 1))
    stacked = jnp.concatenate([left, g, right], axis=0)
    q = jnp.dot(wmat[...], stacked, preferred_element_type=jnp.float32)

    def tap_row(a, b, p, y):
        if not 0 <= y < heights:
            return None
        t = (a * 3 + b) * filters
        c0 = p * plane + y * row
        return q[t:t + filters, c0:c0 + row]

    tiles = []
    for z in range(depth):
        for y in range(heights):
            total = None
            for a in range(3):
                p = z + a - 1
                if not 0 <= p < depth:
                    continue
                for b in range(3):
                    v = tap_row(a, b, p, y + b - 1)
                    if v is not None:
                        total = v if total is None else total + v
            tiles.append(total)
    return jnp.concatenate(tiles, axis=1)


def finish_kernel(acc_ref, p_ref, b_ref, o_ref, *, plane, row, depth):
    filters = acc_ref.shape[0]
    heights = plane // row
    acc = [[acc_ref[:, pl.ds((z * heights + y) * row, row)] for y in range(heights)]
           for z in range(depth)]
    below = p_ref[0]
    above = p_ref[1]
    acc[0] = [v + below[:, y * row:(y + 1) * row] for y, v in enumerate(acc[0])]
    acc[depth - 1] = [v + above[:, y * row:(y + 1) * row] for y, v in enumerate(acc[depth - 1])]
    pooled = []
    for zp in range(depth // 2):
        zmax = [jnp.maximum(u, v) for u, v in zip(acc[2 * zp], acc[2 * zp + 1])]
        for yp in range(heights // 2):
            pooled.append(jnp.maximum(zmax[2 * yp], zmax[2 * yp + 1]))
    m = jnp.concatenate(pooled, axis=1)
    m = jnp.maximum(m, pltpu.roll(m, m.shape[1] - 1, 1))
    brow = jnp.broadcast_to(b_ref[...].astype(jnp.float32), (filters, filters))
    r16 = lax.broadcasted_iota(jnp.int32, (filters, filters), 0)
    c16 = lax.broadcasted_iota(jnp.int32, (filters, filters), 1)
    bias = jnp.sum(jnp.where(r16 == c16, brow, 0.0), axis=1, keepdims=True)
    v = m + bias
    v = jnp.where(v > 0, v, slope * v).astype(jnp.bfloat16)
    r = lax.broadcasted_iota(jnp.int32, (m.shape[1], m.shape[1] // 2), 0)
    c = lax.broadcasted_iota(jnp.int32, (m.shape[1], m.shape[1] // 2), 1)
    pick = (r == 2 * c).astype(jnp.bfloat16)
    picked = jnp.dot(v, pick, preferred_element_type=jnp.float32).astype(o_ref.dtype)
    half = row // 2
    for zp in range(o_ref.shape[1]):
        for yp in range(o_ref.shape[2]):
            k = zp * o_ref.shape[2] + yp
            o_ref[:, zp, yp, :] = picked[:, k * half:(k + 1) * half]


def on_device(volume, kernel, filter_bias):
    local_in, depth, height, across = volume.shape
    weights = kernel.transpose(1, 2, 3, 0, 4)
    return gather_filt(volume, weights, filter_bias.reshape(1, -1))


def solution(mesh):
    in_specs = (P("filt", "space", None, None), P("filt", None, None, None, None), P("filt"))
    out_specs = P("filt", "space", None, None)
    return jax.shard_map(
        on_device, mesh=mesh, in_specs=in_specs, out_specs=out_specs, check_vma=False
    )
```
